32 devices in a mesh: groups: 2 (over y), along: 4 (over z), cross: 2 (over x), sub: 2 (over core).
Axes of the slice: x: 2, y: 2, z: 4, core: 2. Of those that a mesh axis runs over, the one named last changes fastest.
Arguments:
- state_zero: float32 [12, 64, 512], P(None, ('groups', 'along'), ('cross', 'sub')), parts along dimension 1, may hold values from -6 to 6
- storm_field: float32 [12, 64, 512], P(None, ('groups', 'along'), ('cross', 'sub')), parts along dimension 1, may hold values from -6 to 6
- wet_mask: int32 [2, 64, 512], P(None, ('groups', 'along'), ('cross', 'sub')), parts along dimension 1, may hold values 0 or 1
- dune_mask: int32 [2, 64, 512], P(None, ('groups', 'along'), ('cross', 'sub')), parts along dimension 1, may hold values 0 or 1
- class_ids: int32 [64, 512], P(('groups', 'along'), ('cross', 'sub')), parts along dimension 0, may hold values from 0 to 7
- w_one: float32 [32, 128], replicated, may hold values from -1 to 1
- b_one: float32 [128], replicated, may hold values from -3 to 3
- w_two: float32 [128, 128], replicated, may hold values from -0.5 to 0.5
- b_two: float32 [128], replicated, may hold values from -3 to 3
- w_out: float32 [128, 8], replicated, may hold values from -0.5 to 0.5
- b_out: float32 [8], replicated, may hold values from -3 to 3
- final_cotangent: float32 [12, 64, 512], P(None, ('groups', 'along'), ('cross', 'sub')), parts along dimension 1, may hold values from -6 to 6
Outputs:
- grad_state: float32 [12, 64, 512], P(None, ('groups', 'along'), ('cross', 'sub')), parts along dimension 1
- grad_w_one: float32 [64, 128], P('groups'), parts along dimension 0
- grad_b_one: float32 [256], P('groups'), parts along dimension 0
- grad_w_two: float32 [256, 128], P('groups'), parts along dimension 0
- grad_b_two: float32 [256], P('groups'), parts along dimension 0
- grad_w_out: float32 [256, 8], P('groups'), parts along dimension 0
- grad_b_out: float32 [16], P('groups'), parts along dimension 0
The draws below stay inside these ranges and needn't reach their ends.
There are 2 independent parts, one for each index of `groups`. The reference program is written for one: setup_inputs(seed, part) draws one part's arguments, and reference() takes and returns one part's arrays. A program takes and returns all parts, laid end to end along the dimension named above; an argument that names none is the same for every part. Nothing has to cross between parts.
All inputs are finite; a program needn't handle non-finite values. No bound on the sum of `wet_mask` or of `dune_mask` on one device may be relied on, other than what follows from the above.
Results may differ from the reference program's by a relative error of at most 0.0001.
Values sent between devices are 32-bit elements; how exact they have to be, the bound alone decides.
A program may use at most 64 MiB of HBM per device.

```python
import math
import jax
import jax.numpy as jnp
from jax import lax

FIELDS = 12
FEAT = 32
HIDDEN_SIZE = 128
CLASSES = 8
STORM = 12
STEPS = 2
NA = 32
NC = 512


def touch_ends(array, stream_key, smallest, high):
    index_at = [jax.random.randint(jax.random.fold_in(stream_key, axis), (), 0, length) for axis, length in enumerate(array.shape)]
    main_axis = array.shape.index(max(array.shape))
    neighbour = index_at[:main_axis] + [(index_at[main_axis] + 1) % array.shape[main_axis]] + index_at[main_axis + 1:]
    return array.at[tuple(index_at)].set(smallest).at[tuple(neighbour)].set(high)


def block_levels(stream_key, shape, shards, smallest, top_value):
    factor_of = 1.0
    for position, parts in shards:
        draws = jax.random.uniform(jax.random.fold_in(jax.random.fold_in(stream_key, 6), position), (parts,), jnp.float32, smallest / len(shards), top_value / len(shards))
        factor_of = factor_of * jnp.repeat(jnp.exp(draws), shape[position] // parts).reshape((-1,) + (1,) * (len(shape) - 1 - position))
    return factor_of


def centred(own_key, shape, deviation, limit, pieces=(), kind=jnp.bfloat16):
    entries = deviation * jax.random.normal(own_key, shape, jnp.float32)
    if pieces:
        entries = entries * block_levels(own_key, shape, pieces, -0.22, 0.18)
    return jnp.clip(entries, -limit, limit).astype(kind)


def setup_inputs(seed: int = 0, part: int = 0) -> dict:
    arg_keys = jax.random.split(jax.random.key(seed), 13)
    part_splits = jax.random.split(jax.random.fold_in(arg_keys[12], part), 13)
    return {
        "state_zero": centred(part_splits[0], (FIELDS, NA, NC), 1.0, 6.0, ((1, 4), (2, 4)), jnp.float32),
        "storm_field": centred(part_splits[1], (STORM, NA, NC), 1.0, 6.0, ((1, 4), (2, 4)), jnp.float32),
        "wet_mask": touch_ends((jax.random.randint(part_splits[2], (STEPS, NA, NC), 0, 4) < 3).astype(jnp.int32), jax.random.fold_in(part_splits[2], 1), 0, 1),
        "dune_mask": touch_ends((jax.random.randint(part_splits[3], (STEPS, NA, NC), 0, 4) < 1).astype(jnp.int32), jax.random.fold_in(part_splits[3], 1), 0, 1),
        "class_ids": touch_ends(jax.random.randint(part_splits[4], (NA, NC), 0, CLASSES), jax.random.fold_in(part_splits[4], 1), 0, CLASSES - 1).astype(jnp.int32),
        "w_one": centred(arg_keys[5], (FEAT, HIDDEN_SIZE), FEAT ** -0.5, 1.0, (), jnp.float32),
        "b_one": centred(arg_keys[6], (HIDDEN_SIZE,), 0.5, 3.0, (), jnp.float32),
        "w_two": centred(arg_keys[7], (HIDDEN_SIZE, HIDDEN_SIZE), HIDDEN_SIZE ** -0.5, 0.5, (), jnp.float32),
        "b_two": centred(arg_keys[8], (HIDDEN_SIZE,), 0.5, 3.0, (), jnp.float32),
        "w_out": centred(arg_keys[9], (HIDDEN_SIZE, CLASSES), HIDDEN_SIZE ** -0.5, 0.5, (), jnp.float32),
        "b_out": centred(arg_keys[10], (CLASSES,), 0.5, 3.0, (), jnp.float32),
        "final_cotangent": centred(part_splits[11], (FIELDS, NA, NC), 1.0, 6.0, ((1, 4), (2, 4)), jnp.float32),
    }


highest = lax.Precision.HIGHEST
diffusion = 0.15
advection = 0.2
friction = 0.05
pickup_gain = 0.5
settling = 0.2
bed_diffusion = 0.1

def layer_stack(weights, features):
    w_one, b_one, w_two, b_two, w_out, b_out = weights
    hidden_one = jax.nn.silu(jnp.einsum('fh,frc->hrc', w_one, features, precision=highest) + b_one[:, None, None])
    hidden_two = jax.nn.silu(jnp.einsum('hk,hrc->krc', w_two, hidden_one, precision=highest) + b_two[:, None, None])
    return jnp.einsum('ko,krc->orc', w_out, hidden_two, precision=highest) + b_out[:, None, None]

def closure(weights, features, block_rows):
    stack_fn = jax.checkpoint(layer_stack)
    total_rows = features.shape[1]
    if total_rows <= block_rows:
        return stack_fn(weights, features)
    covered = total_rows // block_rows * block_rows
    stacked = jnp.moveaxis(features[:, :covered].reshape(features.shape[0], covered // block_rows, block_rows, features.shape[2]), 1, 0)

    def one_block(block_piece):
        return stack_fn(weights, block_piece)
    mapped = lax.map(one_block, stacked)
    result = jnp.moveaxis(mapped, 0, 1).reshape(mapped.shape[1], covered, features.shape[2])
    if total_rows > covered:
        result = jnp.concatenate([result, stack_fn(weights, features[:, covered:])], axis=1)
    return result

def advance(weights, padded, wet_cells, dune_cells, class_cells, storm_cells, block_rows):
    centre = padded[:, 1:-1, 1:-1]
    north_cells = padded[:, :-2, 1:-1]
    south_cells = padded[:, 2:, 1:-1]
    west_cells = padded[:, 1:-1, :-2]
    east_cells = padded[:, 1:-1, 2:]
    features = jnp.concatenate([centre[:4], north_cells[:4], south_cells[:4], west_cells[:4], east_cells[:4], storm_cells], axis=0)
    outputs = closure(weights, features, block_rows)
    chooser = (class_cells.astype(jnp.float32)[None] == jnp.arange(outputs.shape[0], dtype=jnp.float32)[:, None, None]).astype(jnp.float32)
    pickup = jax.nn.softplus(lax.optimization_barrier(jnp.sum(outputs * chooser, axis=0))) * (1.0 - dune_cells)
    laplace = north_cells + south_cells + west_cells + east_cells - 4.0 * centre
    along_diff = south_cells - north_cells
    cross_diff = east_cells - west_cells
    sediment = centre[4:]
    depth_tend = diffusion * laplace[0] - advection * (along_diff[1] + cross_diff[2])
    along_tend = diffusion * laplace[1] - advection * along_diff[0] - friction * centre[1]
    cross_tend = diffusion * laplace[2] - advection * cross_diff[0] - friction * centre[2]
    bed_tend = bed_diffusion * laplace[3] - pickup_gain * pickup + settling * lax.optimization_barrier(jnp.sum(sediment, axis=0))
    sediment_tend = diffusion * laplace[4:] - advection * (centre[1] * along_diff[4:] + centre[2] * cross_diff[4:]) + pickup_gain * pickup * chooser - settling * sediment
    tendency = jnp.concatenate([jnp.stack([depth_tend, along_tend, cross_tend, bed_tend]), sediment_tend], axis=0)
    return centre + wet_cells[None] * tendency

def reference(state_zero, storm_field, wet_mask, dune_mask, class_ids, w_one, b_one, w_two, b_two, w_out, b_out, final_cotangent):
    weights = (w_one, b_one, w_two, b_two, w_out, b_out)
    wet_float = wet_mask.astype(jnp.float32)
    dune_float = dune_mask.astype(jnp.float32)

    def unrolled(start, params):
        current = start
        for step_index in range(STEPS):
            padded = jnp.pad(current, ((0, 0), (1, 1), (1, 1)))
            current = advance(params, padded, wet_float[step_index], dune_float[step_index], class_ids, storm_field, 8)
        return current
    final_state, pullback = jax.vjp(unrolled, state_zero, weights)
    grad_state, grads = pullback(final_cotangent)
    factor = 1.0 / math.sqrt(state_zero.shape[1] * state_zero.shape[2])
    return (grad_state, grads[0] * factor, grads[1] * factor, grads[2] * factor, grads[3] * factor, grads[4] * factor, grads[5] * factor)
```

```python
import functools
import math

import jax
import jax.numpy as jnp
from jax import lax
from jax.experimental import pallas as pl
from jax.experimental.pallas import tpu as pltpu
from jax.sharding import PartitionSpec as P

MESH = pl.DeviceIdType.MESH
f32 = jnp.float32
bf16 = jnp.bfloat16
diffusion = 0.15
advection = 0.2
friction = 0.05
pickup_gain = 0.5
settling = 0.2
bed_diffusion = 0.1

ROW_B1 = 32
ROW_W2 = 40
ROW_B2 = 168
ROW_WO = 176
ROW_BO = 184
PACK_ROWS = 192
LANES = 256
CHUNKS = 4


def split(x):
    high = x.astype(bf16)
    low = (x - high.astype(f32)).astype(bf16)
    return high, low


def mm(a, b):
    return lax.dot_general(a, b, (((1,), (0,)), ((), ())), preferred_element_type=f32)


def mm_nt(a, b):
    return lax.dot_general(a, b, (((1,), (1,)), ((), ())), preferred_element_type=f32)


def kernel(
    nal, ncr, nsu, chunk_rows, factor,
    state_ref, storm_ref, wet_ref, dune_ref, cid_ref,
    w1_ref, b1_ref, w2_ref, b2_ref, wo_ref, bo_ref, cot_ref,
    gstate_ref, gw1_ref, gb1_ref, gw2_ref, gb2_ref, gwo_ref, gbo_ref,
    snd_row, snd_col, rcv_row, rcv_col, send_sem, recv_sem,
    feat_ref, dfeat_ref, z_ref, dz_ref,
    b1b_ref, b2b_ref, wsel_ref,
    fh_ref, fl_ref, h1h_ref, h1l_ref, h2h_ref, h2l_ref,
    act1_ref, q2_ref, d1h_ref, d1l_ref, d2h_ref, d2l_ref, drh_ref, drl_ref,
    acc_ref, rcv_a, src_b, rcv_b, full_ref,
    sa_send, sa_recv, sb_send, sb_recv, sc_send, sc_recv,
):
    ncs = ncr * nsu
    g = lax.axis_index("groups")
    al = lax.axis_index("along")
    cr = lax.axis_index("cross")
    su = lax.axis_index("sub")
    cs = cr * nsu + su

    def dev(a, c):
        return (g, a, c // nsu, c % nsu)

    has_dst = (al > 0, al < nal - 1, cs > 0, cs < ncs - 1)
    has_src = (al < nal - 1, al > 0, cs < ncs - 1, cs > 0)
    dst_dev = (
        dev(al - 1, cs), dev(al + 1, cs), dev(al, cs - 1), dev(al, cs + 1),
    )

    rcv_row[...] = jnp.zeros_like(rcv_row)
    rcv_col[...] = jnp.zeros_like(rcv_col)

    barrier = pltpu.get_barrier_semaphore()
    for j in range(1, ncs):
        pl.semaphore_signal(
            barrier, inc=1, device_id=dev(al, lax.rem(cs + j, ncs)), device_id_type=MESH
        )
    for j in range(1, nal):
        pl.semaphore_signal(
            barrier, inc=1, device_id=dev(lax.rem(al + j, nal), cs), device_id_type=MESH
        )

    row = lax.broadcasted_iota(jnp.int32, (8, 128), 0)
    lane = lax.broadcasted_iota(jnp.int32, (8, 128), 1)

    def copy_of(k, d):
        if d < 2:
            src, dst = snd_row.at[k, d], rcv_row.at[k, d]
        else:
            src, dst = snd_col.at[k, d - 2], rcv_col.at[k, d - 2]
        return pltpu.make_async_remote_copy(
            src_ref=src, dst_ref=dst, send_sem=send_sem.at[k, d], recv_sem=recv_sem.at[k, d],
            device_id=dst_dev[d], device_id_type=MESH,
        )

    def fill(k, xn, xs, xw, xe):
        west = jnp.zeros((8, 128), f32)
        east = jnp.zeros((8, 128), f32)
        for f in range(12):
            snd_row[k, 0, f:f + 1, :] = xn[f][0:1, :]
            snd_row[k, 1, f:f + 1, :] = xs[f][7:8, :]
            west = jnp.where(lane == f, pltpu.roll(xw[f], f, 1) if f else xw[f], west)
            east = jnp.where(lane == f, pltpu.roll(xe[f], f + 1, 1), east)
        snd_col[k, 0] = west
        snd_col[k, 1] = east

    def launch(k):
        for d in range(4):
            @pl.when(has_dst[d])
            def _():
                copy_of(k, d).start()

    def finish(k):
        for d in range(4):
            @pl.when(has_src[d])
            def _():
                copy_of(k, d).wait_recv()

    def finish_sends(k):
        for d in range(4):
            @pl.when(has_dst[d])
            def _():
                copy_of(k, d).wait_send()

    def south_of(x, f, k):
        return jnp.where(row == 7, rcv_row[k, 0, f:f + 1, :], pltpu.roll(x, 7, 0))

    def north_of(x, f, k):
        return jnp.where(row == 0, rcv_row[k, 1, f:f + 1, :], pltpu.roll(x, 1, 0))

    def east_of(x, f, k):
        return jnp.where(lane == 127, pltpu.roll(rcv_col[k, 0], 127 - f, 1), pltpu.roll(x, 127, 1))

    def west_of(x, f, k):
        halo = rcv_col[k, 1]
        return jnp.where(lane == 0, pltpu.roll(halo, 128 - f, 1) if f else halo, pltpu.roll(x, 1, 1))

    V0 = [state_ref[f] for f in range(12)]
    fill(0, V0, V0, V0, V0)
    pl.semaphore_wait(barrier, ncs - 1 + nal - 1)
    launch(0)

    w1 = w1_ref[...]
    w1t = jnp.transpose(jnp.concatenate([w1, jnp.zeros((96, 128), f32)], axis=0))[:, :32]
    w1th, w1tl = split(w1t)
    w1t_cat = jnp.concatenate([w1th, w1tl, w1th], axis=1)
    w1h, w1l = split(w1)
    w1_hh = jnp.concatenate([w1h, w1h], axis=1)
    w2 = w2_ref[...]
    w2h, w2l = split(w2)
    w2_hh = jnp.concatenate([w2h, w2h], axis=1)
    w2th, w2tl = split(jnp.transpose(w2))
    w2t_hh = jnp.concatenate([w2th, w2th], axis=1)
    b1b_ref[...] = jnp.transpose(jnp.broadcast_to(b1_ref[...], (128, 128)))
    b2b_ref[...] = jnp.transpose(jnp.broadcast_to(b2_ref[...], (128, 128)))
    cid = cid_ref[...]
    wo = wo_ref[...]
    for r in range(8):
        onehot = (lax.broadcasted_iota(jnp.int32, (8, 128), 0) == cid[r:r + 1, :]).astype(f32)
        wsel_ref[:, r * 128:(r + 1) * 128] = lax.dot_general(
            wo, onehot, (((1,), (0,)), ((), ())),
            precision=lax.Precision.HIGHEST, preferred_element_type=f32,
        )
    bsel = jnp.zeros((8, 128), f32)
    for k in range(8):
        bsel = jnp.where(cid == k, bo_ref[k], bsel)
    for f in range(12):
        feat_ref[(20 + f) * 8:(21 + f) * 8, :] = storm_ref[f]
    wets = [wet_ref[t].astype(f32) for t in range(2)]
    wash = [1.0 - dune_ref[t].astype(f32) for t in range(2)]

    def forward(t, V, k):
        near = []
        for f in range(12):
            n, s = north_of(V[f], f, k), south_of(V[f], f, k)
            w, e = west_of(V[f], f, k), east_of(V[f], f, k)
            near.append((n, s, w, e))
            if f < 4:
                feat_ref[f * 8:(f + 1) * 8, :] = V[f]
                feat_ref[(4 + f) * 8:(5 + f) * 8, :] = n
                feat_ref[(8 + f) * 8:(9 + f) * 8, :] = s
                feat_ref[(12 + f) * 8:(13 + f) * 8, :] = w
                feat_ref[(16 + f) * 8:(17 + f) * 8, :] = e
        for c in range(CHUNKS):
            at = pl.ds(c * LANES, LANES)
            F = jnp.concatenate(
                [feat_ref[pl.ds(2 * c + i, 32, stride=8), :] for i in range(2)], axis=1
            )
            Fh, Fl = split(F)
            fh_ref[t, :, at] = Fh
            fl_ref[t, :, at] = Fl
            v = mm(w1t_cat, jnp.concatenate([Fh, Fh, Fl], axis=0))
            bias = b1b_ref[...]
            v = v + jnp.concatenate([bias, bias], axis=1)
            sig = 1.0 / (1.0 + jnp.exp(-v))
            h = v * sig
            act1_ref[t, :, at] = sig + h * (1.0 - sig)
            Hh, Hl = split(h)
            h1h_ref[t, :, at] = Hh
            h1l_ref[t, :, at] = Hl
            v = mm(w2t_hh, jnp.concatenate([Hh, Hl], axis=0)) + mm(w2tl, Hh)
            bias = b2b_ref[...]
            v = v + jnp.concatenate([bias, bias], axis=1)
            sig = 1.0 / (1.0 + jnp.exp(-v))
            h = v * sig
            wsel = wsel_ref[:, at]
            q2_ref[t, :, at] = wsel * (sig + h * (1.0 - sig))
            z = jnp.sum(wsel * h, axis=0, keepdims=True)
            Hh, Hl = split(h)
            h2h_ref[t, :, at] = Hh
            h2l_ref[t, :, at] = Hl
            for i in range(2):
                z_ref[2 * c + i:2 * c + i + 1, :] = z[:, i * 128:(i + 1) * 128]
        return near, z_ref[...] + bsel

    def backward(t, z, near, V, lam):
        G = [wets[t] * lam[f] for f in range(12)]
        picked = G[4]
        for k in range(1, 8):
            picked = jnp.where(cid == k, G[4 + k], picked)
        gate = 1.0 / (1.0 + jnp.exp(-z))
        dz = pickup_gain * (picked - G[3]) * wash[t] * gate
        dz_ref[...] = dz
        for c in range(CHUNKS):
            at = pl.ds(c * LANES, LANES)
            drow = jnp.concatenate(
                [dz_ref[2 * c + i:2 * c + i + 1, :] for i in range(2)], axis=1
            )
            d2 = q2_ref[t, :, at] * drow
            Dh, Dl = split(d2)
            d2h_ref[t, :, at] = Dh
            d2l_ref[t, :, at] = Dl
            d1 = mm(w2_hh, jnp.concatenate([Dh, Dl], axis=0)) + mm(w2l, Dh)
            d1 = d1 * act1_ref[t, :, at]
            Dh, Dl = split(d1)
            d1h_ref[t, :, at] = Dh
            d1l_ref[t, :, at] = Dl
            dF = mm(w1_hh, jnp.concatenate([Dh, Dl], axis=0)) + mm(w1l, Dh)
            for i in range(2):
                dfeat_ref[pl.ds(2 * c + i, 32, stride=8), :] = dF[:, i * 128:(i + 1) * 128]
        D = [dfeat_ref[f * 8:(f + 1) * 8, :] for f in range(20)]
        lap = [bed_diffusion if f == 3 else diffusion for f in range(12)]
        lg = [lap[f] * G[f] for f in range(12)]
        c = [lam[f] - 4.0 * lg[f] for f in range(12)]
        alongs = jnp.zeros((8, 128), f32)
        crosses = jnp.zeros((8, 128), f32)
        along_part = [advection * G[1], advection * G[0], None, None]
        cross_part = [advection * G[2], None, advection * G[0], None]
        for k in range(8):
            n, s, w, e = near[4 + k]
            alongs = alongs + (s - n) * G[4 + k]
            crosses = crosses + (e - w) * G[4 + k]
            c[4 + k] = c[4 + k] + settling * (G[3] - G[4 + k])
            ag = advection * G[4 + k]
            along_part.append(V[1] * ag)
            cross_part.append(V[2] * ag)
        c[1] = c[1] - friction * G[1] - advection * alongs
        c[2] = c[2] - friction * G[2] - advection * crosses
        to = [[], [], [], []]
        for f in range(12):
            for d, part, sign in ((0, along_part, 1), (1, along_part, -1), (2, cross_part, 1), (3, cross_part, -1)):
                x = lg[f]
                if part[f] is not None:
                    x = x + part[f] if sign > 0 else x - part[f]
                if f < 4:
                    x = x + D[4 + 4 * d + f]
                to[d].append(x)
            if f < 4:
                c[f] = c[f] + D[f]
        return dz, c, to

    def gather(c, to, k):
        return [
            c[f] + south_of(to[0][f], f, k) + north_of(to[1][f], f, k)
            + east_of(to[2][f], f, k) + west_of(to[3][f], f, k)
            for f in range(12)
        ]

    def weight_grads(t, dz, first):
        ones = jnp.ones((16, 1024), bf16)
        chooser_rows = []
        for r in range(8):
            onehot = lax.broadcasted_iota(jnp.int32, (8, 128), 0) == cid[r:r + 1, :]
            chooser_rows.append(jnp.where(onehot, dz[r:r + 1, :], 0.0))
        dr = jnp.concatenate(chooser_rows, axis=1)
        dbo = jnp.broadcast_to(jnp.sum(dr, axis=1, keepdims=True), (8, 128))
        pad = jnp.zeros((8, 1024), f32)
        drh, drl = split(jnp.concatenate([dr, pad], axis=0))
        h2h, h2l = h2h_ref[t], h2l_ref[t]
        top = mm_nt(jnp.concatenate([drh, drl], axis=0), h2h)
        dwo = top[:8] + top[16:24] + mm_nt(drh, h2l)[:8]
        lhs = jnp.concatenate([h1h_ref[t], ones, h1l_ref[t]], axis=0)
        top = mm_nt(lhs, d2h_ref[t])
        low = mm_nt(lhs[:144], d2l_ref[t])
        dw2 = top[:128] + top[144:272] + low[:128]
        db2 = top[128:136] + low[128:136]
        lhs = jnp.concatenate([fh_ref[t], ones, fl_ref[t]], axis=0)
        top = mm_nt(lhs, d1h_ref[t])
        low = mm_nt(lhs[:48], d1l_ref[t])
        dw1 = top[:32] + top[48:80] + low[:32]
        db1 = top[32:40] + low[32:40]
        for start, part in ((0, dw1), (ROW_B1, db1), (ROW_W2, dw2), (ROW_B2, db2), (ROW_WO, dwo), (ROW_BO, dbo)):
            at = pl.ds(start, part.shape[0])
            acc_ref[at, :] = part if first else acc_ref[at, :] + part

    finish(0)
    near0, z0 = forward(0, V0, 0)
    soft = jnp.maximum(z0, 0.0) + jnp.log(1.0 + jnp.exp(-jnp.abs(z0)))
    pickup = soft * wash[0]
    V1 = []
    lap = []
    for f in range(12):
        n, s, w, e = near0[f]
        lap.append(n + s + w + e - 4.0 * V0[f])
    total = V0[4]
    for k in range(1, 8):
        total = total + V0[4 + k]
    ad = [near0[f][1] - near0[f][0] for f in range(12)]
    cd = [near0[f][3] - near0[f][2] for f in range(12)]
    tend = [
        diffusion * lap[0] - advection * (ad[1] + cd[2]),
        diffusion * lap[1] - advection * ad[0] - friction * V0[1],
        diffusion * lap[2] - advection * cd[0] - friction * V0[2],
        bed_diffusion * lap[3] - pickup_gain * pickup + settling * total,
    ]
    for k in range(8):
        x = diffusion * lap[4 + k] - advection * (V0[1] * ad[4 + k] + V0[2] * cd[4 + k])
        x = x + jnp.where(cid == k, pickup_gain * pickup, 0.0) - settling * V0[4 + k]
        tend.append(x)
    V1 = [V0[f] + wets[0] * tend[f] for f in range(12)]
    fill(1, V1, V1, V1, V1)
    launch(1)
    finish(1)

    near1, z1 = forward(1, V1, 1)
    lam2 = [cot_ref[f] for f in range(12)]
    dz1, c1, to1 = backward(1, z1, near1, V1, lam2)
    fill(2, *to1)
    launch(2)
    weight_grads(1, dz1, True)
    finish(2)
    lam1 = gather(c1, to1, 2)

    dz0, c0, to0 = backward(0, z0, near0, V0, lam1)
    fill(3, *to0)
    launch(3)
    weight_grads(0, dz0, False)

    def copy_a(j):
        peer = lax.rem(cs + j, ncs)
        return pltpu.make_async_remote_copy(
            src_ref=acc_ref.at[pl.ds(pl.multiple_of(peer * chunk_rows, 8), chunk_rows), :],
            dst_ref=rcv_a.at[j], send_sem=sa_send.at[j], recv_sem=sa_recv.at[j],
            device_id=dev(al, peer), device_id_type=MESH,
        )

    def copy_b(j):
        return pltpu.make_async_remote_copy(
            src_ref=src_b, dst_ref=rcv_b.at[al], send_sem=sb_send.at[j], recv_sem=sb_recv.at[j],
            device_id=dev(lax.rem(al + j, nal), cs), device_id_type=MESH,
        )

    mine = pl.ds(pl.multiple_of(cs * chunk_rows, 8), chunk_rows)

    def copy_c(j):
        return pltpu.make_async_remote_copy(
            src_ref=full_ref.at[mine, :], dst_ref=full_ref.at[mine, :],
            send_sem=sc_send.at[j], recv_sem=sc_recv.at[j],
            device_id=dev(al, lax.rem(cs + j, ncs)), device_id_type=MESH,
        )

    for j in range(1, ncs):
        copy_a(j).start()
    finish(3)
    last = gather(c0, to0, 3)
    for f in range(12):
        gstate_ref[f] = last[f]
    total = acc_ref[mine, :]
    for j in range(1, ncs):
        copy_a(j).wait_recv()
        total = total + rcv_a[j]
    src_b[...] = total
    rcv_b[al] = total
    for j in range(1, nal):
        copy_b(j).start()
    for j in range(1, nal):
        copy_b(j).wait_recv()
    total = rcv_b[0]
    for j in range(1, nal):
        total = total + rcv_b[j]
    full_ref[mine, :] = total * factor
    for j in range(1, ncs):
        copy_c(j).start()
    for j in range(1, ncs):
        copy_c(j).wait_recv()
    gw1_ref[...] = full_ref[0:32, :]
    gb1_ref[...] = full_ref[ROW_B1:ROW_B1 + 1, :]
    gw2_ref[...] = full_ref[ROW_W2:ROW_W2 + 128, :]
    gb2_ref[...] = full_ref[ROW_B2:ROW_B2 + 1, :]
    tail = jnp.concatenate([full_ref[ROW_WO:ROW_BO + 8, :], jnp.zeros((112, 128), f32)], axis=0)
    turned = jnp.transpose(tail)
    gwo_ref[...] = turned[:, :8]
    gbo_ref[...] = turned[0:1, 8:16]
    for k in range(4):
        finish_sends(k)
    for j in range(1, ncs):
        copy_a(j).wait_send()
        copy_c(j).wait_send()
    for j in range(1, nal):
        copy_b(j).wait_send()


def solution(mesh):
    nal, ncr, nsu = mesh.shape["along"], mesh.shape["cross"], mesh.shape["sub"]
    ncs = ncr * nsu
    chunk_rows = 8 * (-(-PACK_ROWS // (8 * ncs)))
    total_rows = chunk_rows * ncs

    def per_device(state, storm, wet, dune, cid, w1, b1, w2, b2, wo, bo, cot):
        rows, cols = state.shape[1], state.shape[2]
        factor = 1.0 / math.sqrt(rows * nal * cols * ncs)
        vmem = pl.BlockSpec(memory_space=pltpu.VMEM)
        smem = pl.BlockSpec(memory_space=pltpu.SMEM)
        dma = pltpu.SemaphoreType.DMA
        big = lambda n, kind: pltpu.VMEM((2, n, 1024), kind)
        out = pl.pallas_call(
            functools.partial(kernel, nal, ncr, nsu, chunk_rows, factor),
            out_shape=(
                jax.ShapeDtypeStruct((12, 8, 128), f32),
                jax.ShapeDtypeStruct((32, 128), f32),
                jax.ShapeDtypeStruct((1, 128), f32),
                jax.ShapeDtypeStruct((128, 128), f32),
                jax.ShapeDtypeStruct((1, 128), f32),
                jax.ShapeDtypeStruct((128, 8), f32),
                jax.ShapeDtypeStruct((1, 8), f32),
            ),
            in_specs=[vmem] * 10 + [smem, vmem],
            out_specs=(vmem,) * 7,
            scratch_shapes=[
                pltpu.VMEM((4, 2, 16, 128), f32),
                pltpu.VMEM((4, 2, 8, 128), f32),
                pltpu.VMEM((4, 2, 16, 128), f32),
                pltpu.VMEM((4, 2, 8, 128), f32),
                dma((4, 4)), dma((4, 4)),
                pltpu.VMEM((256, 128), f32),
                pltpu.VMEM((256, 128), f32),
                pltpu.VMEM((8, 128), f32),
                pltpu.VMEM((8, 128), f32),
                pltpu.VMEM((128, 128), f32),
                pltpu.VMEM((128, 128), f32),
                pltpu.VMEM((128, 1024), f32),
                big(32, bf16), big(32, bf16), big(128, bf16), big(128, bf16), big(128, bf16), big(128, bf16),
                big(128, f32), big(128, f32), big(128, bf16), big(128, bf16), big(128, bf16), big(128, bf16),
                pltpu.VMEM((16, 1024), bf16), pltpu.VMEM((16, 1024), bf16),
                pltpu.VMEM((total_rows, 128), f32),
                pltpu.VMEM((ncs, chunk_rows, 128), f32),
                pltpu.VMEM((chunk_rows, 128), f32),
                pltpu.VMEM((nal, chunk_rows, 128), f32),
                pltpu.VMEM((total_rows, 128), f32),
                dma((ncs,)), dma((ncs,)), dma((nal,)), dma((nal,)), dma((ncs,)), dma((ncs,)),
            ],
            compiler_params=pltpu.CompilerParams(collective_id=0, has_side_effects=True),
        )(state, storm, wet, dune, cid, w1, b1.reshape(1, 128), w2, b2.reshape(1, 128), wo, bo, cot)
        gs, gw1, gb1, gw2, gb2, gwo, gbo = out
        return gs, gw1, gb1.reshape(128), gw2, gb2.reshape(128), gwo, gbo.reshape(8)

    tile = P(None, ("groups", "along"), ("cross", "sub"))
    return jax.shard_map(
        per_device,
        mesh=mesh,
        in_specs=(
            tile, tile, tile, tile, P(("groups", "along"), ("cross", "sub")),
            P(), P(), P(), P(), P(), P(), tile,
        ),
        out_specs=(
            tile, P("groups", None), P("groups"), P("groups", None), P("groups"),
            P("groups", None), P("groups"),
        ),
        check_vma=False,
    )
```

```python
import functools
import math

import jax
import jax.numpy as jnp
from jax import lax
from jax.experimental import pallas as pl
from jax.experimental.pallas import tpu as pltpu
from jax.sharding import PartitionSpec as P

MESH = pl.DeviceIdType.MESH
f32 = jnp.float32
bf16 = jnp.bfloat16
diffusion = 0.15
advection = 0.2
friction = 0.05
pickup_gain = 0.5
settling = 0.2
bed_diffusion = 0.1

ROW_B1 = 32
ROWS_ONE = 40
ROW_B2 = 128
ROW_WO = 136
ROW_BO = 144
ROWS_TWO = 152
LANES = 256
CHUNKS = 4


def split(x):
    high = x.astype(bf16)
    low = (x - high.astype(f32)).astype(bf16)
    return high, low


def mm(a, b):
    return lax.dot_general(a, b, (((1,), (0,)), ((), ())), preferred_element_type=f32)


def mm_nt(a, b):
    return lax.dot_general(a, b, (((1,), (1,)), ((), ())), preferred_element_type=f32)


def kernel(
    nal, ncr, nsu, factor,
    state_ref, storm_ref, wet_ref, dune_ref, cid_ref,
    w1_ref, b1_ref, w2_ref, b2_ref, wo_ref, bo_ref, cot_ref,
    gstate_ref, full_one, full_two,
    snd_row, snd_col, rcv_row, rcv_col, send_sem, recv_sem,
    feat_ref, dfeat_ref, z_ref, dz_ref,
    b1b_ref, b2b_ref, wsel_ref,
    fh_ref, fl_ref, h1h_ref, h1l_ref, h2h_ref, h2l_ref,
    act1_ref, q2_ref, d1h_ref, d1l_ref, d2h_ref, d2l_ref, drh_ref, drl_ref,
    acc_one, rcv_a_one, src_b_one, rcv_b_one, dst_one,
    acc_two, rcv_a_two, src_b_two, rcv_b_two, dst_two,
    sa_send, sa_recv, sb_send, sb_recv, sc_send, sc_recv,
):
    ncs = ncr * nsu
    g = lax.axis_index("groups")
    al = lax.axis_index("along")
    cr = lax.axis_index("cross")
    su = lax.axis_index("sub")
    cs = cr * nsu + su

    def dev(a, c):
        return (g, a, c // nsu, c % nsu)

    has_dst = (al > 0, al < nal - 1, cs > 0, cs < ncs - 1)
    has_src = (al < nal - 1, al > 0, cs < ncs - 1, cs > 0)
    dst_dev = (
        dev(al - 1, cs), dev(al + 1, cs), dev(al, cs - 1), dev(al, cs + 1),
    )

    rcv_row[...] = jnp.zeros_like(rcv_row)
    rcv_col[...] = jnp.zeros_like(rcv_col)

    barrier = pltpu.get_barrier_semaphore()
    for j in range(1, ncs):
        pl.semaphore_signal(
            barrier, inc=1, device_id=dev(al, lax.rem(cs + j, ncs)), device_id_type=MESH
        )
    for j in range(1, nal):
        pl.semaphore_signal(
            barrier, inc=1, device_id=dev(lax.rem(al + j, nal), cs), device_id_type=MESH
        )

    row = lax.broadcasted_iota(jnp.int32, (8, 128), 0)
    lane = lax.broadcasted_iota(jnp.int32, (8, 128), 1)

    def copy_of(k, d):
        if d < 2:
            src, dst = snd_row.at[k, d], rcv_row.at[k, d]
        else:
            src, dst = snd_col.at[k, d - 2], rcv_col.at[k, d - 2]
        return pltpu.make_async_remote_copy(
            src_ref=src, dst_ref=dst, send_sem=send_sem.at[k, d], recv_sem=recv_sem.at[k, d],
            device_id=dst_dev[d], device_id_type=MESH,
        )

    def fill(k, xn, xs, xw, xe):
        west = jnp.zeros((8, 128), f32)
        east = jnp.zeros((8, 128), f32)
        for f in range(12):
            snd_row[k, 0, f:f + 1, :] = xn[f][0:1, :]
            snd_row[k, 1, f:f + 1, :] = xs[f][7:8, :]
            west = jnp.where(lane == f, pltpu.roll(xw[f], f, 1) if f else xw[f], west)
            east = jnp.where(lane == f, pltpu.roll(xe[f], f + 1, 1), east)
        snd_col[k, 0] = west
        snd_col[k, 1] = east

    def launch(k):
        for d in range(4):
            @pl.when(has_dst[d])
            def _():
                copy_of(k, d).start()

    def finish(k):
        for d in range(4):
            @pl.when(has_src[d])
            def _():
                copy_of(k, d).wait_recv()

    def finish_sends(k):
        for d in range(4):
            @pl.when(has_dst[d])
            def _():
                copy_of(k, d).wait_send()

    def south_of(x, f, k):
        return jnp.where(row == 7, rcv_row[k, 0, f:f + 1, :], pltpu.roll(x, 7, 0))

    def north_of(x, f, k):
        return jnp.where(row == 0, rcv_row[k, 1, f:f + 1, :], pltpu.roll(x, 1, 0))

    def east_of(x, f, k):
        return jnp.where(lane == 127, pltpu.roll(rcv_col[k, 0], 127 - f, 1), pltpu.roll(x, 127, 1))

    def west_of(x, f, k):
        halo = rcv_col[k, 1]
        return jnp.where(lane == 0, pltpu.roll(halo, 128 - f, 1) if f else halo, pltpu.roll(x, 1, 1))

    V0 = [state_ref[f] for f in range(12)]
    fill(0, V0, V0, V0, V0)
    pl.semaphore_wait(barrier, ncs - 1 + nal - 1)
    launch(0)

    w1 = w1_ref[...]
    w1t = jnp.transpose(jnp.concatenate([w1, jnp.zeros((96, 128), f32)], axis=0))[:, :32]
    w1th, w1tl = split(w1t)
    w1t_cat = jnp.concatenate([w1th, w1tl, w1th], axis=1)
    w1h, w1l = split(w1)
    w1_hh = jnp.concatenate([w1h, w1h], axis=1)
    w2 = w2_ref[...]
    w2h, w2l = split(w2)
    w2_hh = jnp.concatenate([w2h, w2h], axis=1)
    w2th, w2tl = split(jnp.transpose(w2))
    w2t_hh = jnp.concatenate([w2th, w2th], axis=1)
    b1b_ref[...] = jnp.transpose(jnp.broadcast_to(b1_ref[...], (128, 128)))
    b2b_ref[...] = jnp.transpose(jnp.broadcast_to(b2_ref[...], (128, 128)))
    cid = cid_ref[...]
    wo = wo_ref[...]
    wo_t = jnp.transpose(jnp.concatenate([wo, jnp.zeros((120, 128), f32)], axis=0))[:, :8]
    for r in range(8):
        onehot = (lax.broadcasted_iota(jnp.int32, (8, 128), 0) == cid[r:r + 1, :]).astype(f32)
        wsel_ref[:, r * 128:(r + 1) * 128] = lax.dot_general(
            wo_t, onehot, (((1,), (0,)), ((), ())),
            precision=lax.Precision.HIGHEST, preferred_element_type=f32,
        )
    bsel = jnp.zeros((8, 128), f32)
    for k in range(8):
        bsel = jnp.where(cid == k, bo_ref[k], bsel)
    for f in range(12):
        feat_ref[(20 + f) * 8:(21 + f) * 8, :] = storm_ref[f]
    wets = [wet_ref[t].astype(f32) for t in range(2)]
    wash = [1.0 - dune_ref[t].astype(f32) for t in range(2)]

    def forward(t, V, k):
        near = []
        for f in range(12):
            n, s = north_of(V[f], f, k), south_of(V[f], f, k)
            w, e = west_of(V[f], f, k), east_of(V[f], f, k)
            near.append((n, s, w, e))
            if f < 4:
                feat_ref[f * 8:(f + 1) * 8, :] = V[f]
                feat_ref[(4 + f) * 8:(5 + f) * 8, :] = n
                feat_ref[(8 + f) * 8:(9 + f) * 8, :] = s
                feat_ref[(12 + f) * 8:(13 + f) * 8, :] = w
                feat_ref[(16 + f) * 8:(17 + f) * 8, :] = e
        for c in range(CHUNKS):
            at = pl.ds(c * LANES, LANES)
            F = jnp.concatenate(
                [feat_ref[pl.ds(2 * c + i, 32, stride=8), :] for i in range(2)], axis=1
            )
            Fh, Fl = split(F)
            fh_ref[t, :, at] = Fh
            fl_ref[t, :, at] = Fl
            v = mm(w1t_cat, jnp.concatenate([Fh, Fh, Fl], axis=0))
            bias = b1b_ref[...]
            v = v + jnp.concatenate([bias, bias], axis=1)
            sig = 1.0 / (1.0 + jnp.exp(-v))
            h = v * sig
            act1_ref[t, :, at] = sig + h * (1.0 - sig)
            Hh, Hl = split(h)
            h1h_ref[t, :, at] = Hh
            h1l_ref[t, :, at] = Hl
            v = mm(w2t_hh, jnp.concatenate([Hh, Hl], axis=0)) + mm(w2tl, Hh)
            bias = b2b_ref[...]
            v = v + jnp.concatenate([bias, bias], axis=1)
            sig = 1.0 / (1.0 + jnp.exp(-v))
            h = v * sig
            wsel = wsel_ref[:, at]
            q2_ref[t, :, at] = wsel * (sig + h * (1.0 - sig))
            z = jnp.sum(wsel * h, axis=0, keepdims=True)
            Hh, Hl = split(h)
            h2h_ref[t, :, at] = Hh
            h2l_ref[t, :, at] = Hl
            for i in range(2):
                z_ref[2 * c + i:2 * c + i + 1, :] = z[:, i * 128:(i + 1) * 128]
        return near, z_ref[...] + bsel

    def adjoint_two(t, z, lam):
        G = [wets[t] * lam[f] for f in range(12)]
        picked = G[4]
        for k in range(1, 8):
            picked = jnp.where(cid == k, G[4 + k], picked)
        gate = 1.0 / (1.0 + jnp.exp(-z))
        dz = pickup_gain * (picked - G[3]) * wash[t] * gate
        dz_ref[...] = dz
        for c in range(CHUNKS):
            at = pl.ds(c * LANES, LANES)
            drow = jnp.concatenate(
                [dz_ref[2 * c + i:2 * c + i + 1, :] for i in range(2)], axis=1
            )
            Dh, Dl = split(q2_ref[t, :, at] * drow)
            d2h_ref[t, :, at] = Dh
            d2l_ref[t, :, at] = Dl
        return G, dz

    def adjoint_one(t):
        for c in range(CHUNKS):
            at = pl.ds(c * LANES, LANES)
            Dh, Dl = d2h_ref[t, :, at], d2l_ref[t, :, at]
            d1 = mm(w2_hh, jnp.concatenate([Dh, Dl], axis=0)) + mm(w2l, Dh)
            Dh, Dl = split(d1 * act1_ref[t, :, at])
            d1h_ref[t, :, at] = Dh
            d1l_ref[t, :, at] = Dl

    def adjoint_cells(t, G, near, V, lam):
        for c in range(CHUNKS):
            at = pl.ds(c * LANES, LANES)
            Dh, Dl = d1h_ref[t, :, at], d1l_ref[t, :, at]
            dF = mm(w1_hh, jnp.concatenate([Dh, Dl], axis=0)) + mm(w1l, Dh)
            for i in range(2):
                dfeat_ref[pl.ds(2 * c + i, 32, stride=8), :] = dF[:, i * 128:(i + 1) * 128]
        D = [dfeat_ref[f * 8:(f + 1) * 8, :] for f in range(20)]
        lap = [bed_diffusion if f == 3 else diffusion for f in range(12)]
        lg = [lap[f] * G[f] for f in range(12)]
        c = [lam[f] - 4.0 * lg[f] for f in range(12)]
        alongs = jnp.zeros((8, 128), f32)
        crosses = jnp.zeros((8, 128), f32)
        along_part = [advection * G[1], advection * G[0], None, None]
        cross_part = [advection * G[2], None, advection * G[0], None]
        for k in range(8):
            n, s, w, e = near[4 + k]
            alongs = alongs + (s - n) * G[4 + k]
            crosses = crosses + (e - w) * G[4 + k]
            c[4 + k] = c[4 + k] + settling * (G[3] - G[4 + k])
            ag = advection * G[4 + k]
            along_part.append(V[1] * ag)
            cross_part.append(V[2] * ag)
        c[1] = c[1] - friction * G[1] - advection * alongs
        c[2] = c[2] - friction * G[2] - advection * crosses
        to = [[], [], [], []]
        for f in range(12):
            for d, part, sign in ((0, along_part, 1), (1, along_part, -1), (2, cross_part, 1), (3, cross_part, -1)):
                x = lg[f]
                if part[f] is not None:
                    x = x + part[f] if sign > 0 else x - part[f]
                if f < 4:
                    x = x + D[4 + 4 * d + f]
                to[d].append(x)
            if f < 4:
                c[f] = c[f] + D[f]
        return c, to

    def gather(c, to, k):
        return [
            c[f] + south_of(to[0][f], f, k) + north_of(to[1][f], f, k)
            + east_of(to[2][f], f, k) + west_of(to[3][f], f, k)
            for f in range(12)
        ]

    def keep(ref, start, part, first):
        at = pl.ds(start, part.shape[0])
        ref[at, :] = part if first else ref[at, :] + part

    def weights_two(t, dz, first):
        chooser_rows = []
        for r in range(8):
            onehot = lax.broadcasted_iota(jnp.int32, (8, 128), 0) == cid[r:r + 1, :]
            chooser_rows.append(jnp.where(onehot, dz[r:r + 1, :], 0.0))
        dr = jnp.concatenate(chooser_rows, axis=1)
        dbo = jnp.broadcast_to(jnp.sum(dr, axis=1, keepdims=True), (8, 128))
        pad = jnp.zeros((8, 1024), f32)
        drh, drl = split(jnp.concatenate([dr, pad], axis=0))
        top = mm_nt(jnp.concatenate([drh, drl], axis=0), h2h_ref[t])
        dwo = top[:8] + top[16:24] + mm_nt(drh, h2l_ref[t])[:8]
        lhs = jnp.concatenate([h1h_ref[t], jnp.ones((16, 1024), bf16), h1l_ref[t]], axis=0)
        top = mm_nt(lhs, d2h_ref[t])
        low = mm_nt(lhs[:144], d2l_ref[t])
        keep(acc_two, 0, top[:128] + top[144:272] + low[:128], first)
        keep(acc_two, ROW_B2, top[128:136] + low[128:136], first)
        keep(acc_two, ROW_WO, dwo, first)
        keep(acc_two, ROW_BO, dbo, first)

    def weights_one(t, first):
        lhs = jnp.concatenate([fh_ref[t], jnp.ones((16, 1024), bf16), fl_ref[t]], axis=0)
        top = mm_nt(lhs, d1h_ref[t])
        low = mm_nt(lhs[:48], d1l_ref[t])
        keep(acc_one, 0, top[:32] + top[48:80] + low[:32], first)
        keep(acc_one, ROW_B1, top[32:40] + low[32:40], first)

    finish(0)
    near0, z0 = forward(0, V0, 0)
    soft = jnp.maximum(z0, 0.0) + jnp.log(1.0 + jnp.exp(-jnp.abs(z0)))
    pickup = soft * wash[0]
    V1 = []
    lap = []
    for f in range(12):
        n, s, w, e = near0[f]
        lap.append(n + s + w + e - 4.0 * V0[f])
    total = V0[4]
    for k in range(1, 8):
        total = total + V0[4 + k]
    ad = [near0[f][1] - near0[f][0] for f in range(12)]
    cd = [near0[f][3] - near0[f][2] for f in range(12)]
    tend = [
        diffusion * lap[0] - advection * (ad[1] + cd[2]),
        diffusion * lap[1] - advection * ad[0] - friction * V0[1],
        diffusion * lap[2] - advection * cd[0] - friction * V0[2],
        bed_diffusion * lap[3] - pickup_gain * pickup + settling * total,
    ]
    for k in range(8):
        x = diffusion * lap[4 + k] - advection * (V0[1] * ad[4 + k] + V0[2] * cd[4 + k])
        x = x + jnp.where(cid == k, pickup_gain * pickup, 0.0) - settling * V0[4 + k]
        tend.append(x)
    V1 = [V0[f] + wets[0] * tend[f] for f in range(12)]
    fill(1, V1, V1, V1, V1)
    launch(1)
    finish(1)

    near1, z1 = forward(1, V1, 1)
    lam2 = [cot_ref[f] for f in range(12)]
    G1, dz1 = adjoint_two(1, z1, lam2)
    adjoint_one(1)
    c1, to1 = adjoint_cells(1, G1, near1, V1, lam2)
    fill(2, *to1)
    launch(2)
    for ref, used in ((acc_one, ROWS_ONE), (acc_two, ROWS_TWO)):
        if ref.shape[0] > used:
            ref[used:, :] = jnp.zeros((ref.shape[0] - used, 128), f32)
    weights_two(1, dz1, True)
    weights_one(1, True)
    finish(2)
    lam1 = gather(c1, to1, 2)

    class Sum:
        def __init__(self, which, acc, rcv_a, src_b, rcv_b, full):
            self.which, self.acc, self.rcv_a, self.src_b = which, acc, rcv_a, src_b
            self.rcv_b, self.full = rcv_b, full
            self.rows = src_b.shape[0]
            self.mine = pl.ds(pl.multiple_of(cs * self.rows, 8), self.rows)

        def copy_a(self, j):
            peer = lax.rem(cs + j, ncs)
            return pltpu.make_async_remote_copy(
                src_ref=self.acc.at[pl.ds(pl.multiple_of(peer * self.rows, 8), self.rows), :],
                dst_ref=self.rcv_a.at[j],
                send_sem=sa_send.at[self.which, j], recv_sem=sa_recv.at[self.which, j],
                device_id=dev(al, peer), device_id_type=MESH,
            )

        def copy_b(self, j):
            return pltpu.make_async_remote_copy(
                src_ref=self.src_b, dst_ref=self.rcv_b.at[al],
                send_sem=sb_send.at[self.which, j], recv_sem=sb_recv.at[self.which, j],
                device_id=dev(lax.rem(al + j, nal), cs), device_id_type=MESH,
            )

        def copy_c(self, j):
            return pltpu.make_async_remote_copy(
                src_ref=self.full.at[self.mine, :], dst_ref=self.full.at[self.mine, :],
                send_sem=sc_send.at[self.which, j], recv_sem=sc_recv.at[self.which, j],
                device_id=dev(al, lax.rem(cs + j, ncs)), device_id_type=MESH,
            )

        def first(self):
            for j in range(1, ncs):
                self.copy_a(j).start()

        def second(self):
            total = self.acc[self.mine, :]
            for j in range(1, ncs):
                self.copy_a(j).wait_recv()
                total = total + self.rcv_a[j]
            self.src_b[...] = total
            self.rcv_b[al] = total
            for j in range(1, nal):
                self.copy_b(j).start()

        def third(self):
            for j in range(1, nal):
                self.copy_b(j).wait_recv()
            total = self.rcv_b[0]
            for j in range(1, nal):
                total = total + self.rcv_b[j]
            self.full[self.mine, :] = total * factor
            for j in range(1, ncs):
                self.copy_c(j).start()

        def fourth(self):
            for j in range(1, ncs):
                self.copy_c(j).wait_recv()

        def sends(self):
            for j in range(1, ncs):
                self.copy_a(j).wait_send()
                self.copy_c(j).wait_send()
            for j in range(1, nal):
                self.copy_b(j).wait_send()

    sum_two = Sum(0, acc_two, rcv_a_two, src_b_two, rcv_b_two, dst_two)
    sum_one = Sum(1, acc_one, rcv_a_one, src_b_one, rcv_b_one, dst_one)

    G0, dz0 = adjoint_two(0, z0, lam1)
    weights_two(0, dz0, False)
    sum_two.first()
    adjoint_one(0)
    weights_one(0, False)
    sum_one.first()
    sum_two.second()
    c0, to0 = adjoint_cells(0, G0, near0, V0, lam1)
    fill(3, *to0)
    launch(3)
    sum_one.second()
    sum_two.third()
    finish(3)
    last = gather(c0, to0, 3)
    for f in range(12):
        gstate_ref[f] = last[f]
    sum_one.third()
    sum_two.fourth()
    full_two[...] = dst_two[...]
    sum_one.fourth()
    full_one[...] = dst_one[...]
    for k in range(4):
        finish_sends(k)
    sum_two.sends()
    sum_one.sends()


def unpack(state_ref, one_ref, two_ref, gs_ref, gw1_ref, gb1_ref, gw2_ref, gb2_ref, gwo_ref, gbo_ref):
    gs_ref[...] = state_ref[...]
    gw1_ref[...] = one_ref[0:32, :]
    gb1_ref[...] = one_ref[ROW_B1:ROW_B1 + 1, :]
    gw2_ref[...] = two_ref[0:128, :]
    gb2_ref[...] = two_ref[ROW_B2:ROW_B2 + 1, :]
    gwo_ref[...] = two_ref[ROW_WO:ROW_WO + 8, :]
    wide = jnp.concatenate([two_ref[ROW_BO:ROW_BO + 8, :], jnp.zeros((120, 128), f32)], axis=0)
    gbo_ref[...] = jnp.transpose(wide)[0:1, :8]


def solution(mesh):
    nal, ncr, nsu = mesh.shape["along"], mesh.shape["cross"], mesh.shape["sub"]
    ncs = ncr * nsu
    rows_one = 8 * (-(-ROWS_ONE // (8 * ncs)))
    rows_two = 8 * (-(-ROWS_TWO // (8 * ncs)))

    def per_device(state, storm, wet, dune, cid, w1, b1, w2, b2, wo, bo, cot):
        rows, cols = state.shape[1], state.shape[2]
        factor = 1.0 / math.sqrt(rows * nal * cols * ncs)
        vmem = pl.BlockSpec(memory_space=pltpu.VMEM)
        smem = pl.BlockSpec(memory_space=pltpu.SMEM)
        dma = pltpu.SemaphoreType.DMA
        big = lambda n, kind: pltpu.VMEM((2, n, 1024), kind)
        summed = lambda n: [
            pltpu.VMEM((ncs * n, 128), f32),
            pltpu.VMEM((ncs, n, 128), f32),
            pltpu.VMEM((n, 128), f32),
            pltpu.VMEM((nal, n, 128), f32),
            pltpu.VMEM((ncs * n, 128), f32),
        ]
        out = pl.pallas_call(
            functools.partial(kernel, nal, ncr, nsu, factor),
            out_shape=(
                jax.ShapeDtypeStruct((12, 8, 128), f32),
                jax.ShapeDtypeStruct((ncs * rows_one, 128), f32),
                jax.ShapeDtypeStruct((ncs * rows_two, 128), f32),
            ),
            in_specs=[vmem] * 10 + [smem, vmem],
            out_specs=(vmem,) * 3,
            scratch_shapes=[
                pltpu.VMEM((4, 2, 16, 128), f32),
                pltpu.VMEM((4, 2, 8, 128), f32),
                pltpu.VMEM((4, 2, 16, 128), f32),
                pltpu.VMEM((4, 2, 8, 128), f32),
                dma((4, 4)), dma((4, 4)),
                pltpu.VMEM((256, 128), f32),
                pltpu.VMEM((256, 128), f32),
                pltpu.VMEM((8, 128), f32),
                pltpu.VMEM((8, 128), f32),
                pltpu.VMEM((128, 128), f32),
                pltpu.VMEM((128, 128), f32),
                pltpu.VMEM((128, 1024), f32),
                big(32, bf16), big(32, bf16), big(128, bf16), big(128, bf16), big(128, bf16), big(128, bf16),
                big(128, f32), big(128, f32), big(128, bf16), big(128, bf16), big(128, bf16), big(128, bf16),
                pltpu.VMEM((16, 1024), bf16), pltpu.VMEM((16, 1024), bf16),
                *summed(rows_one), *summed(rows_two),
                dma((2, ncs)), dma((2, ncs)), dma((2, nal)), dma((2, nal)), dma((2, ncs)), dma((2, ncs)),
            ],
            compiler_params=pltpu.CompilerParams(collective_id=0, has_side_effects=True),
        )(state, storm, wet, dune, cid, w1, b1.reshape(1, 128), w2, b2.reshape(1, 128), wo.T, bo, cot)
        gs, gw1, gb1, gw2, gb2, gwo, gbo = pl.pallas_call(
            unpack,
            out_shape=(
                jax.ShapeDtypeStruct((12, 8, 128), f32),
                jax.ShapeDtypeStruct((32, 128), f32),
                jax.ShapeDtypeStruct((1, 128), f32),
                jax.ShapeDtypeStruct((128, 128), f32),
                jax.ShapeDtypeStruct((1, 128), f32),
                jax.ShapeDtypeStruct((8, 128), f32),
                jax.ShapeDtypeStruct((1, 8), f32),
            ),
            in_specs=[vmem] * 3,
            out_specs=(vmem,) * 7,
            compiler_params=pltpu.CompilerParams(vmem_limit_bytes=4 << 20),
        )(*out)
        return gs, gw1, gb1.reshape(128), gw2, gb2.reshape(128), gwo.T, gbo.reshape(8)

    tile = P(None, ("groups", "along"), ("cross", "sub"))
    return jax.shard_map(
        per_device,
        mesh=mesh,
        in_specs=(
            tile, tile, tile, tile, P(("groups", "along"), ("cross", "sub")),
            P(), P(), P(), P(), P(), P(), tile,
        ),
        out_specs=(
            tile, P("groups", None), P("groups"), P("groups", None), P("groups"),
            P("groups", None), P("groups"),
        ),
        check_vma=False,
    )
```

```python
import functools
import math

import jax
import jax.numpy as jnp
from jax import lax
from jax.experimental import pallas as pl
from jax.experimental.pallas import tpu as pltpu
from jax.sharding import PartitionSpec as P

MESH = pl.DeviceIdType.MESH
f32 = jnp.float32
bf16 = jnp.bfloat16
diffusion = 0.15
advection = 0.2
friction = 0.05
pickup_gain = 0.5
settling = 0.2
bed_diffusion = 0.1

ROW_B1 = 32
ROWS_ONE = 40
ROW_B2 = 128
ROW_WO = 136
ROW_BO = 144
ROWS_TWO = 152
LANES = 256
CHUNKS = 4


def split(x):
    high = x.astype(bf16)
    low = (x - high.astype(f32)).astype(bf16)
    return high, low


def mm(a, b):
    return lax.dot_general(a, b, (((1,), (0,)), ((), ())), preferred_element_type=f32)


def mm_nt(a, b):
    return lax.dot_general(a, b, (((1,), (1,)), ((), ())), preferred_element_type=f32)


def kernel(
    nal, ncr, nsu, factor,
    state_hbm, cid_hbm, w1_hbm, b1_hbm, w2_hbm, b2_hbm, wo_hbm, bo_hbm,
    storm_hbm, wet_hbm, dune_hbm, cot_hbm,
    gstate_hbm, one_hbm, two_hbm,
    state_ref, cid_ref, w1_ref, b1_ref, w2_ref, b2_ref, wo_ref, bo_ref,
    storm_ref, wet_ref, dune_ref, cot_ref, gstate_ref, load_sem, store_sem,
    snd_row, snd_col, rcv_row, rcv_col, send_sem, recv_sem,
    feat_ref, dfeat_ref, z_ref, dz_ref,
    b1b_ref, b2b_ref, wsel_ref,
    fh_ref, fl_ref, h1h_ref, h1l_ref, h2h_ref, h2l_ref,
    act1_ref, q2_ref, d1h_ref, d1l_ref, d2h_ref, d2l_ref, drh_ref, drl_ref,
    acc_one, rcv_a_one, src_b_one, rcv_b_one, dst_one,
    acc_two, rcv_a_two, src_b_two, rcv_b_two, dst_two,
    sa_send, sa_recv, sb_send, sb_recv, sc_send, sc_recv,
):
    ncs = ncr * nsu
    g = lax.axis_index("groups")
    al = lax.axis_index("along")
    cr = lax.axis_index("cross")
    su = lax.axis_index("sub")
    cs = cr * nsu + su

    def dev(a, c):
        return (g, a, c // nsu, c % nsu)

    has_dst = (al > 0, al < nal - 1, cs > 0, cs < ncs - 1)
    has_src = (al < nal - 1, al > 0, cs < ncs - 1, cs > 0)
    dst_dev = (
        dev(al - 1, cs), dev(al + 1, cs), dev(al, cs - 1), dev(al, cs + 1),
    )

    loads = [
        pltpu.make_async_copy(src, dst, load_sem.at[i])
        for i, (src, dst) in enumerate((
            (state_hbm, state_ref), (cid_hbm, cid_ref), (w1_hbm, w1_ref), (b1_hbm, b1_ref),
            (w2_hbm, w2_ref), (b2_hbm, b2_ref), (wo_hbm, wo_ref), (bo_hbm, bo_ref),
            (storm_hbm, storm_ref), (wet_hbm, wet_ref), (dune_hbm, dune_ref), (cot_hbm, cot_ref),
        ))
    ]
    loads[0].start()
    rcv_row[...] = jnp.zeros_like(rcv_row)
    rcv_col[...] = jnp.zeros_like(rcv_col)

    barrier = pltpu.get_barrier_semaphore()
    near_only = nal <= 4 and ncs <= 4
    if near_only:
        for d in range(4):
            @pl.when(has_dst[d])
            def _():
                pl.semaphore_signal(barrier, inc=1, device_id=dst_dev[d], device_id_type=MESH)
    else:
        for j in range(1, ncs):
            pl.semaphore_signal(
                barrier, inc=1, device_id=dev(al, lax.rem(cs + j, ncs)), device_id_type=MESH
            )
        for j in range(1, nal):
            pl.semaphore_signal(
                barrier, inc=1, device_id=dev(lax.rem(al + j, nal), cs), device_id_type=MESH
            )
    for load in loads[1:]:
        load.start()

    row = lax.broadcasted_iota(jnp.int32, (8, 128), 0)
    lane = lax.broadcasted_iota(jnp.int32, (8, 128), 1)

    def copy_of(k, d):
        if d < 2:
            src, dst = snd_row.at[k, d], rcv_row.at[k, d]
        else:
            src, dst = snd_col.at[k, d - 2], rcv_col.at[k, d - 2]
        return pltpu.make_async_remote_copy(
            src_ref=src, dst_ref=dst, send_sem=send_sem.at[k, d], recv_sem=recv_sem.at[k, d],
            device_id=dst_dev[d], device_id_type=MESH,
        )

    def fill(k, xn, xs, xw, xe):
        west = jnp.zeros((8, 128), f32)
        east = jnp.zeros((8, 128), f32)
        for f in range(12):
            snd_row[k, 0, f:f + 1, :] = xn[f][0:1, :]
            snd_row[k, 1, f:f + 1, :] = xs[f][7:8, :]
            west = jnp.where(lane == f, pltpu.roll(xw[f], f, 1) if f else xw[f], west)
            east = jnp.where(lane == f, pltpu.roll(xe[f], f + 1, 1), east)
        snd_col[k, 0] = west
        snd_col[k, 1] = east

    def launch(k):
        for d in range(4):
            @pl.when(has_dst[d])
            def _():
                copy_of(k, d).start()

    def finish(k):
        for d in range(4):
            @pl.when(has_src[d])
            def _():
                copy_of(k, d).wait_recv()

    def finish_sends(k):
        for d in range(4):
            @pl.when(has_dst[d])
            def _():
                copy_of(k, d).wait_send()

    def south_of(x, f, k):
        return jnp.where(row == 7, rcv_row[k, 0, f:f + 1, :], pltpu.roll(x, 7, 0))

    def north_of(x, f, k):
        return jnp.where(row == 0, rcv_row[k, 1, f:f + 1, :], pltpu.roll(x, 1, 0))

    def east_of(x, f, k):
        return jnp.where(lane == 127, pltpu.roll(rcv_col[k, 0], 127 - f, 1), pltpu.roll(x, 127, 1))

    def west_of(x, f, k):
        halo = rcv_col[k, 1]
        return jnp.where(lane == 0, pltpu.roll(halo, 128 - f, 1) if f else halo, pltpu.roll(x, 1, 1))

    loads[0].wait()
    V0 = [state_ref[f] for f in range(12)]
    fill(0, V0, V0, V0, V0)
    if near_only:
        beside = (al + nal - 1) // nal + (2 * nal - 2 - al) // nal
        beside = beside + (cs + ncs - 1) // ncs + (2 * ncs - 2 - cs) // ncs
        pl.semaphore_wait(barrier, beside)
    else:
        pl.semaphore_wait(barrier, ncs - 1 + nal - 1)
    launch(0)
    for load in loads[1:]:
        load.wait()

    w1 = w1_ref[...]
    w1t = jnp.transpose(jnp.concatenate([w1, jnp.zeros((96, 128), f32)], axis=0))[:, :32]
    w1th, w1tl = split(w1t)
    w1t_cat = jnp.concatenate([w1th, w1tl, w1th], axis=1)
    w1h, w1l = split(w1)
    w1_hh = jnp.concatenate([w1h, w1h], axis=1)
    w2 = w2_ref[...]
    w2h, w2l = split(w2)
    w2_hh = jnp.concatenate([w2h, w2h], axis=1)
    w2th, w2tl = split(jnp.transpose(w2))
    w2t_hh = jnp.concatenate([w2th, w2th], axis=1)
    b1b_ref[...] = jnp.transpose(jnp.broadcast_to(b1_ref[...], (128, 128)))
    b2b_ref[...] = jnp.transpose(jnp.broadcast_to(b2_ref[...], (128, 128)))
    cid = cid_ref[...]
    wo = wo_ref[...]
    wo_t = jnp.transpose(jnp.concatenate([wo, jnp.zeros((120, 128), f32)], axis=0))[:, :8]
    for r in range(8):
        onehot = (lax.broadcasted_iota(jnp.int32, (8, 128), 0) == cid[r:r + 1, :]).astype(f32)
        wsel_ref[:, r * 128:(r + 1) * 128] = lax.dot_general(
            wo_t, onehot, (((1,), (0,)), ((), ())),
            precision=lax.Precision.HIGHEST, preferred_element_type=f32,
        )
    bsel = jnp.zeros((8, 128), f32)
    for k in range(8):
        bsel = jnp.where(cid == k, bo_ref[0:1, k:k + 1], bsel)
    for f in range(12):
        feat_ref[(20 + f) * 8:(21 + f) * 8, :] = storm_ref[f]
    wets = [wet_ref[t].astype(f32) for t in range(2)]
    wash = [1.0 - dune_ref[t].astype(f32) for t in range(2)]

    def forward(t, V, k):
        near = []
        for f in range(12):
            n, s = north_of(V[f], f, k), south_of(V[f], f, k)
            w, e = west_of(V[f], f, k), east_of(V[f], f, k)
            near.append((n, s, w, e))
            if f < 4:
                feat_ref[f * 8:(f + 1) * 8, :] = V[f]
                feat_ref[(4 + f) * 8:(5 + f) * 8, :] = n
                feat_ref[(8 + f) * 8:(9 + f) * 8, :] = s
                feat_ref[(12 + f) * 8:(13 + f) * 8, :] = w
                feat_ref[(16 + f) * 8:(17 + f) * 8, :] = e
        for c in range(CHUNKS):
            at = pl.ds(c * LANES, LANES)
            F = jnp.concatenate(
                [feat_ref[pl.ds(2 * c + i, 32, stride=8), :] for i in range(2)], axis=1
            )
            Fh, Fl = split(F)
            fh_ref[t, :, at] = Fh
            fl_ref[t, :, at] = Fl
            v = mm(w1t_cat, jnp.concatenate([Fh, Fh, Fl], axis=0))
            bias = b1b_ref[...]
            v = v + jnp.concatenate([bias, bias], axis=1)
            sig = 1.0 / (1.0 + jnp.exp(-v))
            h = v * sig
            act1_ref[t, :, at] = sig + h * (1.0 - sig)
            Hh, Hl = split(h)
            h1h_ref[t, :, at] = Hh
            h1l_ref[t, :, at] = Hl
            v = mm(w2t_hh, jnp.concatenate([Hh, Hl], axis=0)) + mm(w2tl, Hh)
            bias = b2b_ref[...]
            v = v + jnp.concatenate([bias, bias], axis=1)
            sig = 1.0 / (1.0 + jnp.exp(-v))
            h = v * sig
            wsel = wsel_ref[:, at]
            q2_ref[t, :, at] = wsel * (sig + h * (1.0 - sig))
            z = jnp.sum(wsel * h, axis=0, keepdims=True)
            Hh, Hl = split(h)
            h2h_ref[t, :, at] = Hh
            h2l_ref[t, :, at] = Hl
            for i in range(2):
                z_ref[2 * c + i:2 * c + i + 1, :] = z[:, i * 128:(i + 1) * 128]
        return near, z_ref[...] + bsel

    def adjoint_two(t, z, lam):
        G = [wets[t] * lam[f] for f in range(12)]
        picked = G[4]
        for k in range(1, 8):
            picked = jnp.where(cid == k, G[4 + k], picked)
        gate = 1.0 / (1.0 + jnp.exp(-z))
        dz = pickup_gain * (picked - G[3]) * wash[t] * gate
        dz_ref[...] = dz
        for c in range(CHUNKS):
            at = pl.ds(c * LANES, LANES)
            drow = jnp.concatenate(
                [dz_ref[2 * c + i:2 * c + i + 1, :] for i in range(2)], axis=1
            )
            Dh, Dl = split(q2_ref[t, :, at] * drow)
            d2h_ref[t, :, at] = Dh
            d2l_ref[t, :, at] = Dl
        return G, dz

    def adjoint_one(t):
        for c in range(CHUNKS):
            at = pl.ds(c * LANES, LANES)
            Dh, Dl = d2h_ref[t, :, at], d2l_ref[t, :, at]
            d1 = mm(w2_hh, jnp.concatenate([Dh, Dl], axis=0)) + mm(w2l, Dh)
            Dh, Dl = split(d1 * act1_ref[t, :, at])
            d1h_ref[t, :, at] = Dh
            d1l_ref[t, :, at] = Dl

    def adjoint_cells(t, G, near, V, lam):
        for c in range(CHUNKS):
            at = pl.ds(c * LANES, LANES)
            Dh, Dl = d1h_ref[t, :, at], d1l_ref[t, :, at]
            dF = mm(w1_hh, jnp.concatenate([Dh, Dl], axis=0)) + mm(w1l, Dh)
            for i in range(2):
                dfeat_ref[pl.ds(2 * c + i, 32, stride=8), :] = dF[:, i * 128:(i + 1) * 128]
        D = [dfeat_ref[f * 8:(f + 1) * 8, :] for f in range(20)]
        lap = [bed_diffusion if f == 3 else diffusion for f in range(12)]
        lg = [lap[f] * G[f] for f in range(12)]
        c = [lam[f] - 4.0 * lg[f] for f in range(12)]
        alongs = jnp.zeros((8, 128), f32)
        crosses = jnp.zeros((8, 128), f32)
        along_part = [advection * G[1], advection * G[0], None, None]
        cross_part = [advection * G[2], None, advection * G[0], None]
        for k in range(8):
            n, s, w, e = near[4 + k]
            alongs = alongs + (s - n) * G[4 + k]
            crosses = crosses + (e - w) * G[4 + k]
            c[4 + k] = c[4 + k] + settling * (G[3] - G[4 + k])
            ag = advection * G[4 + k]
            along_part.append(V[1] * ag)
            cross_part.append(V[2] * ag)
        c[1] = c[1] - friction * G[1] - advection * alongs
        c[2] = c[2] - friction * G[2] - advection * crosses
        to = [[], [], [], []]
        for f in range(12):
            for d, part, sign in ((0, along_part, 1), (1, along_part, -1), (2, cross_part, 1), (3, cross_part, -1)):
                x = lg[f]
                if part[f] is not None:
                    x = x + part[f] if sign > 0 else x - part[f]
                if f < 4:
                    x = x + D[4 + 4 * d + f]
                to[d].append(x)
            if f < 4:
                c[f] = c[f] + D[f]
        return c, to

    def gather(c, to, k):
        return [
            c[f] + south_of(to[0][f], f, k) + north_of(to[1][f], f, k)
            + east_of(to[2][f], f, k) + west_of(to[3][f], f, k)
            for f in range(12)
        ]

    def keep(ref, start, part, first):
        at = pl.ds(start, part.shape[0])
        ref[at, :] = part if first else ref[at, :] + part

    def weights_two(t, dz, first):
        chooser_rows = []
        for r in range(8):
            onehot = lax.broadcasted_iota(jnp.int32, (8, 128), 0) == cid[r:r + 1, :]
            chooser_rows.append(jnp.where(onehot, dz[r:r + 1, :], 0.0))
        dr = jnp.concatenate(chooser_rows, axis=1)
        dbo = jnp.broadcast_to(jnp.sum(dr, axis=1, keepdims=True), (8, 128))
        pad = jnp.zeros((8, 1024), f32)
        drh, drl = split(jnp.concatenate([dr, pad], axis=0))
        top = mm_nt(jnp.concatenate([drh, drl], axis=0), h2h_ref[t])
        dwo = top[:8] + top[16:24] + mm_nt(drh, h2l_ref[t])[:8]
        lhs = jnp.concatenate([h1h_ref[t], jnp.ones((16, 1024), bf16), h1l_ref[t]], axis=0)
        top = mm_nt(lhs, d2h_ref[t])
        low = mm_nt(lhs[:144], d2l_ref[t])
        keep(acc_two, 0, top[:128] + top[144:272] + low[:128], first)
        keep(acc_two, ROW_B2, top[128:136] + low[128:136], first)
        keep(acc_two, ROW_WO, dwo, first)
        keep(acc_two, ROW_BO, dbo, first)

    def weights_one(t, first):
        lhs = jnp.concatenate([fh_ref[t], jnp.ones((16, 1024), bf16), fl_ref[t]], axis=0)
        top = mm_nt(lhs, d1h_ref[t])
        low = mm_nt(lhs[:48], d1l_ref[t])
        keep(acc_one, 0, top[:32] + top[48:80] + low[:32], first)
        keep(acc_one, ROW_B1, top[32:40] + low[32:40], first)

    finish(0)
    near0, z0 = forward(0, V0, 0)
    soft = jnp.maximum(z0, 0.0) + jnp.log(1.0 + jnp.exp(-jnp.abs(z0)))
    pickup = soft * wash[0]
    V1 = []
    lap = []
    for f in range(12):
        n, s, w, e = near0[f]
        lap.append(n + s + w + e - 4.0 * V0[f])
    total = V0[4]
    for k in range(1, 8):
        total = total + V0[4 + k]
    ad = [near0[f][1] - near0[f][0] for f in range(12)]
    cd = [near0[f][3] - near0[f][2] for f in range(12)]
    tend = [
        diffusion * lap[0] - advection * (ad[1] + cd[2]),
        diffusion * lap[1] - advection * ad[0] - friction * V0[1],
        diffusion * lap[2] - advection * cd[0] - friction * V0[2],
        bed_diffusion * lap[3] - pickup_gain * pickup + settling * total,
    ]
    for k in range(8):
        x = diffusion * lap[4 + k] - advection * (V0[1] * ad[4 + k] + V0[2] * cd[4 + k])
        x = x + jnp.where(cid == k, pickup_gain * pickup, 0.0) - settling * V0[4 + k]
        tend.append(x)
    V1 = [V0[f] + wets[0] * tend[f] for f in range(12)]
    fill(1, V1, V1, V1, V1)
    launch(1)
    finish(1)

    near1, z1 = forward(1, V1, 1)
    lam2 = [cot_ref[f] for f in range(12)]
    G1, dz1 = adjoint_two(1, z1, lam2)
    adjoint_one(1)
    c1, to1 = adjoint_cells(1, G1, near1, V1, lam2)
    fill(2, *to1)
    launch(2)
    for ref, used in ((acc_one, ROWS_ONE), (acc_two, ROWS_TWO)):
        if ref.shape[0] > used:
            ref[used:, :] = jnp.zeros((ref.shape[0] - used, 128), f32)
    weights_two(1, dz1, True)
    weights_one(1, True)
    finish(2)
    lam1 = gather(c1, to1, 2)

    class Sum:
        def __init__(self, which, acc, rcv_a, src_b, rcv_b, full):
            self.which, self.acc, self.rcv_a, self.src_b = which, acc, rcv_a, src_b
            self.rcv_b, self.full = rcv_b, full
            self.rows = src_b.shape[0]
            self.mine = pl.ds(pl.multiple_of(cs * self.rows, 8), self.rows)

        def copy_a(self, j):
            peer = lax.rem(cs + j, ncs)
            return pltpu.make_async_remote_copy(
                src_ref=self.acc.at[pl.ds(pl.multiple_of(peer * self.rows, 8), self.rows), :],
                dst_ref=self.rcv_a.at[j],
                send_sem=sa_send.at[self.which, j], recv_sem=sa_recv.at[self.which, j],
                device_id=dev(al, peer), device_id_type=MESH,
            )

        def copy_b(self, j):
            return pltpu.make_async_remote_copy(
                src_ref=self.src_b, dst_ref=self.rcv_b.at[al],
                send_sem=sb_send.at[self.which, j], recv_sem=sb_recv.at[self.which, j],
                device_id=dev(lax.rem(al + j, nal), cs), device_id_type=MESH,
            )

        def copy_c(self, j):
            return pltpu.make_async_remote_copy(
                src_ref=self.full.at[self.mine, :], dst_ref=self.full.at[self.mine, :],
                send_sem=sc_send.at[self.which, j], recv_sem=sc_recv.at[self.which, j],
                device_id=dev(al, lax.rem(cs + j, ncs)), device_id_type=MESH,
            )

        def first(self):
            for j in range(1, ncs):
                self.copy_a(j).start()

        def second(self):
            total = self.acc[self.mine, :]
            for j in range(1, ncs):
                self.copy_a(j).wait_recv()
                total = total + self.rcv_a[j]
            self.src_b[...] = total
            self.rcv_b[al] = total
            for j in range(1, nal):
                self.copy_b(j).start()

        def third(self):
            for j in range(1, nal):
                self.copy_b(j).wait_recv()
            total = self.rcv_b[0]
            for j in range(1, nal):
                total = total + self.rcv_b[j]
            self.full[self.mine, :] = total * factor
            for j in range(1, ncs):
                self.copy_c(j).start()

        def fourth(self):
            for j in range(1, ncs):
                self.copy_c(j).wait_recv()

        def sends(self):
            for j in range(1, ncs):
                self.copy_a(j).wait_send()
                self.copy_c(j).wait_send()
            for j in range(1, nal):
                self.copy_b(j).wait_send()

    sum_two = Sum(0, acc_two, rcv_a_two, src_b_two, rcv_b_two, dst_two)
    sum_one = Sum(1, acc_one, rcv_a_one, src_b_one, rcv_b_one, dst_one)

    G0, dz0 = adjoint_two(0, z0, lam1)
    weights_two(0, dz0, False)
    sum_two.first()
    adjoint_one(0)
    weights_one(0, False)
    sum_one.first()
    sum_two.second()
    c0, to0 = adjoint_cells(0, G0, near0, V0, lam1)
    fill(3, *to0)
    launch(3)
    sum_one.second()
    sum_two.third()
    finish(3)
    last = gather(c0, to0, 3)
    for f in range(12):
        gstate_ref[f] = last[f]
    stores = [
        pltpu.make_async_copy(src, dst, store_sem.at[i])
        for i, (src, dst) in enumerate(
            ((gstate_ref, gstate_hbm), (dst_one, one_hbm), (dst_two, two_hbm))
        )
    ]
    stores[0].start()
    sum_one.third()
    sum_two.fourth()
    stores[2].start()
    sum_one.fourth()
    stores[1].start()
    for k in range(4):
        finish_sends(k)
    sum_two.sends()
    sum_one.sends()
    for store in stores:
        store.wait()


def unpack(state_ref, one_ref, two_ref, gs_ref, gw1_ref, gb1_ref, gw2_ref, gb2_ref, gwo_ref, gbo_ref):
    gs_ref[...] = state_ref[...]
    gw1_ref[...] = one_ref[0:32, :]
    gb1_ref[...] = one_ref[ROW_B1:ROW_B1 + 1, :]
    gw2_ref[...] = two_ref[0:128, :]
    gb2_ref[...] = two_ref[ROW_B2:ROW_B2 + 1, :]
    gwo_ref[...] = two_ref[ROW_WO:ROW_WO + 8, :]
    wide = jnp.concatenate([two_ref[ROW_BO:ROW_BO + 8, :], jnp.zeros((120, 128), f32)], axis=0)
    gbo_ref[...] = jnp.transpose(wide)[0:1, :8]


def solution(mesh):
    nal, ncr, nsu = mesh.shape["along"], mesh.shape["cross"], mesh.shape["sub"]
    ncs = ncr * nsu
    rows_one = 8 * (-(-ROWS_ONE // (8 * ncs)))
    rows_two = 8 * (-(-ROWS_TWO // (8 * ncs)))

    def per_device(state, storm, wet, dune, cid, w1, b1, w2, b2, wo, bo, cot):
        rows, cols = state.shape[1], state.shape[2]
        factor = 1.0 / math.sqrt(rows * nal * cols * ncs)
        vmem = pl.BlockSpec(memory_space=pltpu.VMEM)
        hbm = pl.BlockSpec(memory_space=pl.ANY)
        operands = (
            state, cid, w1, b1.reshape(1, 128), w2, b2.reshape(1, 128), wo.T, bo.reshape(1, 8),
            storm, wet, dune, cot,
        )
        dma = pltpu.SemaphoreType.DMA
        big = lambda n, kind: pltpu.VMEM((2, n, 1024), kind)
        summed = lambda n: [
            pltpu.VMEM((ncs * n, 128), f32),
            pltpu.VMEM((ncs, n, 128), f32),
            pltpu.VMEM((n, 128), f32),
            pltpu.VMEM((nal, n, 128), f32),
            pltpu.VMEM((ncs * n, 128), f32),
        ]
        out = pl.pallas_call(
            functools.partial(kernel, nal, ncr, nsu, factor),
            out_shape=(
                jax.ShapeDtypeStruct((12, 8, 128), f32),
                jax.ShapeDtypeStruct((ncs * rows_one, 128), f32),
                jax.ShapeDtypeStruct((ncs * rows_two, 128), f32),
            ),
            in_specs=[hbm] * 12,
            out_specs=(hbm,) * 3,
            scratch_shapes=[
                *[pltpu.VMEM(x.shape, x.dtype) for x in operands],
                pltpu.VMEM((12, 8, 128), f32), dma((12,)), dma((3,)),
                pltpu.VMEM((4, 2, 16, 128), f32),
                pltpu.VMEM((4, 2, 8, 128), f32),
                pltpu.VMEM((4, 2, 16, 128), f32),
                pltpu.VMEM((4, 2, 8, 128), f32),
                dma((4, 4)), dma((4, 4)),
                pltpu.VMEM((256, 128), f32),
                pltpu.VMEM((256, 128), f32),
                pltpu.VMEM((8, 128), f32),
                pltpu.VMEM((8, 128), f32),
                pltpu.VMEM((128, 128), f32),
                pltpu.VMEM((128, 128), f32),
                pltpu.VMEM((128, 1024), f32),
                big(32, bf16), big(32, bf16), big(128, bf16), big(128, bf16), big(128, bf16), big(128, bf16),
                big(128, f32), big(128, f32), big(128, bf16), big(128, bf16), big(128, bf16), big(128, bf16),
                pltpu.VMEM((16, 1024), bf16), pltpu.VMEM((16, 1024), bf16),
                *summed(rows_one), *summed(rows_two),
                dma((2, ncs)), dma((2, ncs)), dma((2, nal)), dma((2, nal)), dma((2, ncs)), dma((2, ncs)),
            ],
            compiler_params=pltpu.CompilerParams(collective_id=0, has_side_effects=True),
        )(*operands)
        gs, gw1, gb1, gw2, gb2, gwo, gbo = pl.pallas_call(
            unpack,
            out_shape=(
                jax.ShapeDtypeStruct((12, 8, 128), f32),
                jax.ShapeDtypeStruct((32, 128), f32),
                jax.ShapeDtypeStruct((1, 128), f32),
                jax.ShapeDtypeStruct((128, 128), f32),
                jax.ShapeDtypeStruct((1, 128), f32),
                jax.ShapeDtypeStruct((8, 128), f32),
                jax.ShapeDtypeStruct((1, 8), f32),
            ),
            in_specs=[vmem] * 3,
            out_specs=(vmem,) * 7,
        )(*out)
        return gs, gw1, gb1.reshape(128), gw2, gb2.reshape(128), gwo.T, gbo.reshape(8)

    tile = P(None, ("groups", "along"), ("cross", "sub"))
    return jax.shard_map(
        per_device,
        mesh=mesh,
        in_specs=(
            tile, tile, tile, tile, P(("groups", "along"), ("cross", "sub")),
            P(), P(), P(), P(), P(), P(), tile,
        ),
        out_specs=(
            tile, P("groups", None), P("groups"), P("groups", None), P("groups"),
            P("groups", None), P("groups"),
        ),
        check_vma=False,
    )
```

```python
import functools
import math

import jax
import jax.numpy as jnp
from jax import lax
from jax.experimental import pallas as pl
from jax.experimental.pallas import tpu as pltpu
from jax.sharding import PartitionSpec as P

MESH = pl.DeviceIdType.MESH
f32 = jnp.float32
bf16 = jnp.bfloat16
diffusion = 0.15
advection = 0.2
friction = 0.05
pickup_gain = 0.5
settling = 0.2
bed_diffusion = 0.1

ROW_B1 = 32
ROWS_ONE = 40
ROW_B2 = 128
ROW_WO = 136
ROW_BO = 144
ROWS_TWO = 152
LANES = 256
CHUNKS = 4


def split(x):
    high = x.astype(bf16)
    low = (x - high.astype(f32)).astype(bf16)
    return high, low


def mm(a, b):
    return lax.dot_general(a, b, (((1,), (0,)), ((), ())), preferred_element_type=f32)


def mm_nt(a, b):
    return lax.dot_general(a, b, (((1,), (1,)), ((), ())), preferred_element_type=f32)


def kernel(
    nal, ncr, nsu, factor,
    state_hbm, cid_hbm, w1_hbm, b1_hbm, w2_hbm, b2_hbm, wo_hbm, bo_hbm,
    storm_hbm, wet_hbm, dune_hbm, cot_hbm,
    gstate_hbm, one_hbm, two_hbm,
    state_ref, cid_ref, w1_ref, b1_ref, w2_ref, b2_ref, wo_ref, bo_ref,
    storm_ref, wet_ref, dune_ref, cot_ref, gstate_ref, load_sem, store_sem,
    snd_row, snd_col, rcv_row, rcv_col, send_sem, recv_sem,
    feat_ref, dfeat_ref, z_ref, dz_ref,
    b1b_ref, b2b_ref, wsel_ref,
    fh_ref, fl_ref, h1h_ref, h1l_ref, h2h_ref, h2l_ref,
    act1_ref, q2_ref, d1h_ref, d1l_ref, d2h_ref, d2l_ref, drh_ref, drl_ref,
    acc_one, rcv_a_one, src_b_one, rcv_b_one, dst_one,
    acc_two, rcv_a_two, src_b_two, rcv_b_two, dst_two,
    sa_send, sa_recv, sb_send, sb_recv, sc_send, sc_recv,
):
    ncs = ncr * nsu
    g = lax.axis_index("groups")
    al = lax.axis_index("along")
    cr = lax.axis_index("cross")
    su = lax.axis_index("sub")
    cs = cr * nsu + su

    def dev(a, c):
        return (g, a, c // nsu, c % nsu)

    has_dst = (al > 0, al < nal - 1, cs > 0, cs < ncs - 1)
    has_src = (al < nal - 1, al > 0, cs < ncs - 1, cs > 0)
    dst_dev = (
        dev(al - 1, cs), dev(al + 1, cs), dev(al, cs - 1), dev(al, cs + 1),
    )

    loads = [
        pltpu.make_async_copy(src, dst, load_sem.at[i])
        for i, (src, dst) in enumerate((
            (state_hbm, state_ref), (cid_hbm, cid_ref), (w1_hbm, w1_ref), (b1_hbm, b1_ref),
            (w2_hbm, w2_ref), (b2_hbm, b2_ref), (wo_hbm, wo_ref), (bo_hbm, bo_ref),
            (storm_hbm, storm_ref), (wet_hbm, wet_ref), (dune_hbm, dune_ref), (cot_hbm, cot_ref),
        ))
    ]
    loads[0].start()
    rcv_row[...] = jnp.zeros_like(rcv_row)
    rcv_col[...] = jnp.zeros_like(rcv_col)

    barrier = pltpu.get_barrier_semaphore()
    near_only = nal <= 4 and ncs <= 4
    if near_only:
        for d in range(4):
            @pl.when(has_dst[d])
            def _():
                pl.semaphore_signal(barrier, inc=1, device_id=dst_dev[d], device_id_type=MESH)
    else:
        for j in range(1, ncs):
            pl.semaphore_signal(
                barrier, inc=1, device_id=dev(al, lax.rem(cs + j, ncs)), device_id_type=MESH
            )
        for j in range(1, nal):
            pl.semaphore_signal(
                barrier, inc=1, device_id=dev(lax.rem(al + j, nal), cs), device_id_type=MESH
            )
    for load in loads[1:]:
        load.start()

    row = lax.broadcasted_iota(jnp.int32, (8, 128), 0)
    lane = lax.broadcasted_iota(jnp.int32, (8, 128), 1)

    def copy_of(k, d):
        if d < 2:
            src, dst = snd_row.at[k, d], rcv_row.at[k, d]
        else:
            src, dst = snd_col.at[k, d - 2], rcv_col.at[k, d - 2]
        return pltpu.make_async_remote_copy(
            src_ref=src, dst_ref=dst, send_sem=send_sem.at[k, d], recv_sem=recv_sem.at[k, d],
            device_id=dst_dev[d], device_id_type=MESH,
        )

    def fill(k, xn, xs, xw, xe):
        west = jnp.zeros((8, 128), f32)
        east = jnp.zeros((8, 128), f32)
        for f in range(12):
            snd_row[k, 0, f:f + 1, :] = xn[f][0:1, :]
            snd_row[k, 1, f:f + 1, :] = xs[f][7:8, :]
            west = jnp.where(lane == f, pltpu.roll(xw[f], f, 1) if f else xw[f], west)
            east = jnp.where(lane == f, pltpu.roll(xe[f], f + 1, 1), east)
        snd_col[k, 0] = west
        snd_col[k, 1] = east

    def launch(k):
        for d in range(4):
            @pl.when(has_dst[d])
            def _():
                copy_of(k, d).start()

    def finish(k):
        for d in range(4):
            @pl.when(has_src[d])
            def _():
                copy_of(k, d).wait_recv()

    def finish_sends(k):
        for d in range(4):
            @pl.when(has_dst[d])
            def _():
                copy_of(k, d).wait_send()

    def south_of(x, f, k):
        return jnp.where(row == 7, rcv_row[k, 0, f:f + 1, :], pltpu.roll(x, 7, 0))

    def north_of(x, f, k):
        return jnp.where(row == 0, rcv_row[k, 1, f:f + 1, :], pltpu.roll(x, 1, 0))

    def east_of(x, f, k):
        return jnp.where(lane == 127, pltpu.roll(rcv_col[k, 0], 127 - f, 1), pltpu.roll(x, 127, 1))

    def west_of(x, f, k):
        halo = rcv_col[k, 1]
        return jnp.where(lane == 0, pltpu.roll(halo, 128 - f, 1) if f else halo, pltpu.roll(x, 1, 1))

    loads[0].wait()
    V0 = [state_ref[f] for f in range(12)]
    fill(0, V0, V0, V0, V0)
    if near_only:
        beside = (al + nal - 1) // nal + (2 * nal - 2 - al) // nal
        beside = beside + (cs + ncs - 1) // ncs + (2 * ncs - 2 - cs) // ncs
        pl.semaphore_wait(barrier, beside)
    else:
        pl.semaphore_wait(barrier, ncs - 1 + nal - 1)
    launch(0)
    for load in loads[1:]:
        load.wait()

    w1 = w1_ref[...]
    w1t = jnp.transpose(jnp.concatenate([w1, jnp.zeros((96, 128), f32)], axis=0))[:, :32]
    w1th, w1tl = split(w1t)
    w1t_cat = jnp.concatenate([w1th, w1tl, w1th], axis=1)
    w1h, w1l = split(w1)
    w1_hh = jnp.concatenate([w1h, w1h], axis=1)
    w2 = w2_ref[...]
    w2h, w2l = split(w2)
    w2_hh = jnp.concatenate([w2h, w2h], axis=1)
    w2th, w2tl = split(jnp.transpose(w2))
    w2t_hh = jnp.concatenate([w2th, w2th], axis=1)
    b1b_ref[...] = jnp.transpose(jnp.broadcast_to(b1_ref[...], (128, 128)))
    b2b_ref[...] = jnp.transpose(jnp.broadcast_to(b2_ref[...], (128, 128)))
    cid = cid_ref[...]
    wo = wo_ref[...]
    wo_t = jnp.transpose(jnp.concatenate([wo, jnp.zeros((120, 128), f32)], axis=0))[:, :8]
    for r in range(8):
        onehot = (lax.broadcasted_iota(jnp.int32, (8, 128), 0) == cid[r:r + 1, :]).astype(f32)
        wsel_ref[:, r * 128:(r + 1) * 128] = lax.dot_general(
            wo_t, onehot, (((1,), (0,)), ((), ())),
            precision=lax.Precision.HIGHEST, preferred_element_type=f32,
        )
    bsel = jnp.zeros((8, 128), f32)
    for k in range(8):
        bsel = jnp.where(cid == k, bo_ref[0:1, k:k + 1], bsel)
    for f in range(12):
        feat_ref[(20 + f) * 8:(21 + f) * 8, :] = storm_ref[f]
    wets = [wet_ref[t].astype(f32) for t in range(2)]
    wash = [1.0 - dune_ref[t].astype(f32) for t in range(2)]

    def forward(t, V, k):
        near = []
        for f in range(12):
            n, s = north_of(V[f], f, k), south_of(V[f], f, k)
            w, e = west_of(V[f], f, k), east_of(V[f], f, k)
            near.append((n, s, w, e))
            if f < 4:
                feat_ref[f * 8:(f + 1) * 8, :] = V[f]
                feat_ref[(4 + f) * 8:(5 + f) * 8, :] = n
                feat_ref[(8 + f) * 8:(9 + f) * 8, :] = s
                feat_ref[(12 + f) * 8:(13 + f) * 8, :] = w
                feat_ref[(16 + f) * 8:(17 + f) * 8, :] = e
        for c in range(CHUNKS):
            at = pl.ds(c * LANES, LANES)
            F = jnp.concatenate(
                [feat_ref[pl.ds(2 * c + i, 32, stride=8), :] for i in range(2)], axis=1
            )
            Fh, Fl = split(F)
            fh_ref[t, :, at] = Fh
            fl_ref[t, :, at] = Fl
            v = mm(w1t_cat, jnp.concatenate([Fh, Fh, Fl], axis=0))
            bias = b1b_ref[...]
            v = v + jnp.concatenate([bias, bias], axis=1)
            sig = 0.5 + 0.5 * jnp.tanh(0.5 * v)
            h = v * sig
            act1_ref[t, :, at] = sig + h * (1.0 - sig)
            Hh, Hl = split(h)
            h1h_ref[t, :, at] = Hh
            h1l_ref[t, :, at] = Hl
            v = mm(w2t_hh, jnp.concatenate([Hh, Hl], axis=0)) + mm(w2tl, Hh)
            bias = b2b_ref[...]
            v = v + jnp.concatenate([bias, bias], axis=1)
            sig = 0.5 + 0.5 * jnp.tanh(0.5 * v)
            h = v * sig
            wsel = wsel_ref[:, at]
            q2_ref[t, :, at] = wsel * (sig + h * (1.0 - sig))
            z = jnp.sum(wsel * h, axis=0, keepdims=True)
            Hh, Hl = split(h)
            h2h_ref[t, :, at] = Hh
            h2l_ref[t, :, at] = Hl
            for i in range(2):
                z_ref[2 * c + i:2 * c + i + 1, :] = z[:, i * 128:(i + 1) * 128]
        return near, z_ref[...] + bsel

    def adjoint_two(t, z, lam):
        G = [wets[t] * lam[f] for f in range(12)]
        picked = G[4]
        for k in range(1, 8):
            picked = jnp.where(cid == k, G[4 + k], picked)
        gate = 1.0 / (1.0 + jnp.exp(-z))
        dz = pickup_gain * (picked - G[3]) * wash[t] * gate
        dz_ref[...] = dz
        for c in range(CHUNKS):
            at = pl.ds(c * LANES, LANES)
            drow = jnp.concatenate(
                [dz_ref[2 * c + i:2 * c + i + 1, :] for i in range(2)], axis=1
            )
            Dh, Dl = split(q2_ref[t, :, at] * drow)
            d2h_ref[t, :, at] = Dh
            d2l_ref[t, :, at] = Dl
        return G, dz

    def adjoint_one(t):
        for c in range(CHUNKS):
            at = pl.ds(c * LANES, LANES)
            Dh, Dl = d2h_ref[t, :, at], d2l_ref[t, :, at]
            d1 = mm(w2_hh, jnp.concatenate([Dh, Dl], axis=0)) + mm(w2l, Dh)
            Dh, Dl = split(d1 * act1_ref[t, :, at])
            d1h_ref[t, :, at] = Dh
            d1l_ref[t, :, at] = Dl

    def adjoint_cells(t, G, near, V, lam):
        for c in range(CHUNKS):
            at = pl.ds(c * LANES, LANES)
            Dh, Dl = d1h_ref[t, :, at], d1l_ref[t, :, at]
            dF = mm(w1_hh, jnp.concatenate([Dh, Dl], axis=0)) + mm(w1l, Dh)
            for i in range(2):
                dfeat_ref[pl.ds(2 * c + i, 32, stride=8), :] = dF[:, i * 128:(i + 1) * 128]
        D = [dfeat_ref[f * 8:(f + 1) * 8, :] for f in range(20)]
        lap = [bed_diffusion if f == 3 else diffusion for f in range(12)]
        lg = [lap[f] * G[f] for f in range(12)]
        c = [lam[f] - 4.0 * lg[f] for f in range(12)]
        alongs = jnp.zeros((8, 128), f32)
        crosses = jnp.zeros((8, 128), f32)
        along_part = [advection * G[1], advection * G[0], None, None]
        cross_part = [advection * G[2], None, advection * G[0], None]
        for k in range(8):
            n, s, w, e = near[4 + k]
            alongs = alongs + (s - n) * G[4 + k]
            crosses = crosses + (e - w) * G[4 + k]
            c[4 + k] = c[4 + k] + settling * (G[3] - G[4 + k])
            ag = advection * G[4 + k]
            along_part.append(V[1] * ag)
            cross_part.append(V[2] * ag)
        c[1] = c[1] - friction * G[1] - advection * alongs
        c[2] = c[2] - friction * G[2] - advection * crosses
        to = [[], [], [], []]
        for f in range(12):
            for d, part, sign in ((0, along_part, 1), (1, along_part, -1), (2, cross_part, 1), (3, cross_part, -1)):
                x = lg[f]
                if part[f] is not None:
                    x = x + part[f] if sign > 0 else x - part[f]
                if f < 4:
                    x = x + D[4 + 4 * d + f]
                to[d].append(x)
            if f < 4:
                c[f] = c[f] + D[f]
        return c, to

    def gather(c, to, k):
        return [
            c[f] + south_of(to[0][f], f, k) + north_of(to[1][f], f, k)
            + east_of(to[2][f], f, k) + west_of(to[3][f], f, k)
            for f in range(12)
        ]

    def keep(ref, start, part, first):
        at = pl.ds(start, part.shape[0])
        ref[at, :] = part if first else ref[at, :] + part

    def weights_two(t, dz, first):
        chooser_rows = []
        for r in range(8):
            onehot = lax.broadcasted_iota(jnp.int32, (8, 128), 0) == cid[r:r + 1, :]
            chooser_rows.append(jnp.where(onehot, dz[r:r + 1, :], 0.0))
        dr = jnp.concatenate(chooser_rows, axis=1)
        dbo = jnp.broadcast_to(jnp.sum(dr, axis=1, keepdims=True), (8, 128))
        pad = jnp.zeros((8, 1024), f32)
        drh, drl = split(jnp.concatenate([dr, pad], axis=0))
        top = mm_nt(jnp.concatenate([drh, drl], axis=0), h2h_ref[t])
        dwo = top[:8] + top[16:24] + mm_nt(drh, h2l_ref[t])[:8]
        lhs = jnp.concatenate([h1h_ref[t], jnp.ones((16, 1024), bf16), h1l_ref[t]], axis=0)
        top = mm_nt(lhs, d2h_ref[t])
        low = mm_nt(lhs[:144], d2l_ref[t])
        keep(acc_two, 0, top[:128] + top[144:272] + low[:128], first)
        keep(acc_two, ROW_B2, top[128:136] + low[128:136], first)
        keep(acc_two, ROW_WO, dwo, first)
        keep(acc_two, ROW_BO, dbo, first)

    def weights_one(t, first):
        lhs = jnp.concatenate([fh_ref[t], jnp.ones((16, 1024), bf16), fl_ref[t]], axis=0)
        top = mm_nt(lhs, d1h_ref[t])
        low = mm_nt(lhs[:48], d1l_ref[t])
        keep(acc_one, 0, top[:32] + top[48:80] + low[:32], first)
        keep(acc_one, ROW_B1, top[32:40] + low[32:40], first)

    finish(0)
    near0, z0 = forward(0, V0, 0)
    soft = jnp.maximum(z0, 0.0) + jnp.log(1.0 + jnp.exp(-jnp.abs(z0)))
    pickup = soft * wash[0]
    V1 = []
    lap = []
    for f in range(12):
        n, s, w, e = near0[f]
        lap.append(n + s + w + e - 4.0 * V0[f])
    total = V0[4]
    for k in range(1, 8):
        total = total + V0[4 + k]
    ad = [near0[f][1] - near0[f][0] for f in range(12)]
    cd = [near0[f][3] - near0[f][2] for f in range(12)]
    tend = [
        diffusion * lap[0] - advection * (ad[1] + cd[2]),
        diffusion * lap[1] - advection * ad[0] - friction * V0[1],
        diffusion * lap[2] - advection * cd[0] - friction * V0[2],
        bed_diffusion * lap[3] - pickup_gain * pickup + settling * total,
    ]
    for k in range(8):
        x = diffusion * lap[4 + k] - advection * (V0[1] * ad[4 + k] + V0[2] * cd[4 + k])
        x = x + jnp.where(cid == k, pickup_gain * pickup, 0.0) - settling * V0[4 + k]
        tend.append(x)
    V1 = [V0[f] + wets[0] * tend[f] for f in range(12)]
    fill(1, V1, V1, V1, V1)
    launch(1)
    finish(1)

    near1, z1 = forward(1, V1, 1)
    lam2 = [cot_ref[f] for f in range(12)]
    G1, dz1 = adjoint_two(1, z1, lam2)
    adjoint_one(1)
    c1, to1 = adjoint_cells(1, G1, near1, V1, lam2)
    fill(2, *to1)
    launch(2)
    for ref, used in ((acc_one, ROWS_ONE), (acc_two, ROWS_TWO)):
        if ref.shape[0] > used:
            ref[used:, :] = jnp.zeros((ref.shape[0] - used, 128), f32)
    weights_two(1, dz1, True)
    weights_one(1, True)
    finish(2)
    lam1 = gather(c1, to1, 2)

    class Sum:
        def __init__(self, which, acc, rcv_a, src_b, rcv_b, full):
            self.which, self.acc, self.rcv_a, self.src_b = which, acc, rcv_a, src_b
            self.rcv_b, self.full = rcv_b, full
            self.rows = src_b.shape[0]
            self.mine = pl.ds(pl.multiple_of(cs * self.rows, 8), self.rows)

        def copy_a(self, j):
            peer = lax.rem(cs + j, ncs)
            return pltpu.make_async_remote_copy(
                src_ref=self.acc.at[pl.ds(pl.multiple_of(peer * self.rows, 8), self.rows), :],
                dst_ref=self.rcv_a.at[j],
                send_sem=sa_send.at[self.which, j], recv_sem=sa_recv.at[self.which, j],
                device_id=dev(al, peer), device_id_type=MESH,
            )

        def copy_b(self, j):
            return pltpu.make_async_remote_copy(
                src_ref=self.src_b, dst_ref=self.rcv_b.at[al],
                send_sem=sb_send.at[self.which, j], recv_sem=sb_recv.at[self.which, j],
                device_id=dev(lax.rem(al + j, nal), cs), device_id_type=MESH,
            )

        def copy_c(self, j):
            return pltpu.make_async_remote_copy(
                src_ref=self.full.at[self.mine, :], dst_ref=self.full.at[self.mine, :],
                send_sem=sc_send.at[self.which, j], recv_sem=sc_recv.at[self.which, j],
                device_id=dev(al, lax.rem(cs + j, ncs)), device_id_type=MESH,
            )

        def first(self):
            for j in range(1, ncs):
                self.copy_a(j).start()

        def second(self):
            total = self.acc[self.mine, :]
            for j in range(1, ncs):
                self.copy_a(j).wait_recv()
                total = total + self.rcv_a[j]
            self.src_b[...] = total
            self.rcv_b[al] = total
            for j in range(1, nal):
                self.copy_b(j).start()

        def third(self):
            for j in range(1, nal):
                self.copy_b(j).wait_recv()
            total = self.rcv_b[0]
            for j in range(1, nal):
                total = total + self.rcv_b[j]
            self.full[self.mine, :] = total * factor
            for j in range(1, ncs):
                self.copy_c(j).start()

        def fourth(self):
            for j in range(1, ncs):
                self.copy_c(j).wait_recv()

        def sends(self):
            for j in range(1, ncs):
                self.copy_a(j).wait_send()
                self.copy_c(j).wait_send()
            for j in range(1, nal):
                self.copy_b(j).wait_send()

    sum_two = Sum(0, acc_two, rcv_a_two, src_b_two, rcv_b_two, dst_two)
    sum_one = Sum(1, acc_one, rcv_a_one, src_b_one, rcv_b_one, dst_one)

    G0, dz0 = adjoint_two(0, z0, lam1)
    weights_two(0, dz0, False)
    sum_two.first()
    adjoint_one(0)
    weights_one(0, False)
    sum_one.first()
    c0, to0 = adjoint_cells(0, G0, near0, V0, lam1)
    fill(3, *to0)
    launch(3)
    sum_two.second()
    sum_one.second()
    finish(3)
    last = gather(c0, to0, 3)
    for f in range(12):
        gstate_ref[f] = last[f]
    stores = [
        pltpu.make_async_copy(src, dst, store_sem.at[i])
        for i, (src, dst) in enumerate(
            ((gstate_ref, gstate_hbm), (dst_one, one_hbm), (dst_two, two_hbm))
        )
    ]
    stores[0].start()
    sum_two.third()
    sum_one.third()
    sum_two.fourth()
    stores[2].start()
    sum_one.fourth()
    stores[1].start()
    for k in range(4):
        finish_sends(k)
    sum_two.sends()
    sum_one.sends()
    for store in stores:
        store.wait()


def unpack(state_ref, one_ref, two_ref, gs_ref, gw1_ref, gb1_ref, gw2_ref, gb2_ref, gwo_ref, gbo_ref):
    gs_ref[...] = state_ref[...]
    gw1_ref[...] = one_ref[0:32, :]
    gb1_ref[...] = one_ref[ROW_B1:ROW_B1 + 1, :]
    gw2_ref[...] = two_ref[0:128, :]
    gb2_ref[...] = two_ref[ROW_B2:ROW_B2 + 1, :]
    gwo_ref[...] = two_ref[ROW_WO:ROW_WO + 8, :]
    wide = jnp.concatenate([two_ref[ROW_BO:ROW_BO + 8, :], jnp.zeros((120, 128), f32)], axis=0)
    gbo_ref[...] = jnp.transpose(wide)[0:1, :8]


def solution(mesh):
    nal, ncr, nsu = mesh.shape["along"], mesh.shape["cross"], mesh.shape["sub"]
    ncs = ncr * nsu
    rows_one = 8 * (-(-ROWS_ONE // (8 * ncs)))
    rows_two = 8 * (-(-ROWS_TWO // (8 * ncs)))

    def per_device(state, storm, wet, dune, cid, w1, b1, w2, b2, wo, bo, cot):
        rows, cols = state.shape[1], state.shape[2]
        factor = 1.0 / math.sqrt(rows * nal * cols * ncs)
        vmem = pl.BlockSpec(memory_space=pltpu.VMEM)
        hbm = pl.BlockSpec(memory_space=pl.ANY)
        operands = (
            state, cid, w1, b1.reshape(1, 128), w2, b2.reshape(1, 128), wo.T, bo.reshape(1, 8),
            storm, wet, dune, cot,
        )
        dma = pltpu.SemaphoreType.DMA
        big = lambda n, kind: pltpu.VMEM((2, n, 1024), kind)
        summed = lambda n: [
            pltpu.VMEM((ncs * n, 128), f32),
            pltpu.VMEM((ncs, n, 128), f32),
            pltpu.VMEM((n, 128), f32),
            pltpu.VMEM((nal, n, 128), f32),
            pltpu.VMEM((ncs * n, 128), f32),
        ]
        out = pl.pallas_call(
            functools.partial(kernel, nal, ncr, nsu, factor),
            out_shape=(
                jax.ShapeDtypeStruct((12, 8, 128), f32),
                jax.ShapeDtypeStruct((ncs * rows_one, 128), f32),
                jax.ShapeDtypeStruct((ncs * rows_two, 128), f32),
            ),
            in_specs=[hbm] * 12,
            out_specs=(hbm,) * 3,
            scratch_shapes=[
                *[pltpu.VMEM(x.shape, x.dtype) for x in operands],
                pltpu.VMEM((12, 8, 128), f32), dma((12,)), dma((3,)),
                pltpu.VMEM((4, 2, 16, 128), f32),
                pltpu.VMEM((4, 2, 8, 128), f32),
                pltpu.VMEM((4, 2, 16, 128), f32),
                pltpu.VMEM((4, 2, 8, 128), f32),
                dma((4, 4)), dma((4, 4)),
                pltpu.VMEM((256, 128), f32),
                pltpu.VMEM((256, 128), f32),
                pltpu.VMEM((8, 128), f32),
                pltpu.VMEM((8, 128), f32),
                pltpu.VMEM((128, 128), f32),
                pltpu.VMEM((128, 128), f32),
                pltpu.VMEM((128, 1024), f32),
                big(32, bf16), big(32, bf16), big(128, bf16), big(128, bf16), big(128, bf16), big(128, bf16),
                big(128, f32), big(128, f32), big(128, bf16), big(128, bf16), big(128, bf16), big(128, bf16),
                pltpu.VMEM((16, 1024), bf16), pltpu.VMEM((16, 1024), bf16),
                *summed(rows_one), *summed(rows_two),
                dma((2, ncs)), dma((2, ncs)), dma((2, nal)), dma((2, nal)), dma((2, ncs)), dma((2, ncs)),
            ],
            compiler_params=pltpu.CompilerParams(collective_id=0, has_side_effects=True),
        )(*operands)
        gs, gw1, gb1, gw2, gb2, gwo, gbo = pl.pallas_call(
            unpack,
            out_shape=(
                jax.ShapeDtypeStruct((12, 8, 128), f32),
                jax.ShapeDtypeStruct((32, 128), f32),
                jax.ShapeDtypeStruct((1, 128), f32),
                jax.ShapeDtypeStruct((128, 128), f32),
                jax.ShapeDtypeStruct((1, 128), f32),
                jax.ShapeDtypeStruct((8, 128), f32),
                jax.ShapeDtypeStruct((1, 8), f32),
            ),
            in_specs=[vmem] * 3,
            out_specs=(vmem,) * 7,
        )(*out)
        return gs, gw1, gb1.reshape(128), gw2, gb2.reshape(128), gwo.T, gbo.reshape(8)

    tile = P(None, ("groups", "along"), ("cross", "sub"))
    return jax.shard_map(
        per_device,
        mesh=mesh,
        in_specs=(
            tile, tile, tile, tile, P(("groups", "along"), ("cross", "sub")),
            P(), P(), P(), P(), P(), P(), tile,
        ),
        out_specs=(
            tile, P("groups", None), P("groups"), P("groups", None), P("groups"),
            P("groups", None), P("groups"),
        ),
        check_vma=False,
    )
```
